256 devices in a mesh: seq: 64 (over z_hi, y, x, core), tp: 4 (over z_lo).
Axes of the slice: x: 4, y: 4, z: 8 (z_hi: 2, z_lo: 4; z = z_hi * 4 + z_lo), core: 2. Of those that a mesh axis runs over, the one named last changes fastest.
Arguments:
- tokens: bfloat16 [8192, 2048], P(('seq', 'tp')), may hold values from -6 to 6
- block_ids: int32 [64, 2], replicated, may hold values from 0 to 127, as said below
- attn_gain: float32 [2048], replicated, may hold values from 0.25 to 1.75
- q_weight: bfloat16 [2048, 3072], P(None, 'tp'), may hold values from -0.125 to 0.125
- kv_weight: bfloat16 [2048, 576], replicated, may hold values from -0.125 to 0.125
- kv_gain: float32 [512], replicated, may hold values from 0.25 to 1.75
- uk_weight: bfloat16 [16, 512, 128], P('tp'), may hold values from -40 to 40
- uv_weight: bfloat16 [16, 512, 128], P('tp'), may hold values from -0.25 to 0.25
- o_weight: bfloat16 [2048, 2048], P('tp'), may hold values from -0.125 to 0.125
- ffn_gain: float32 [2048], replicated, may hold values from 0.25 to 1.75
- w_gate: bfloat16 [64, 2048, 1408], P('seq', None, 'tp'), may hold values from -0.125 to 0.125
- w_up: bfloat16 [64, 2048, 1408], P('seq', None, 'tp'), may hold values from -0.125 to 0.125
- w_down: bfloat16 [64, 1408, 2048], P('seq', 'tp'), may hold values from -0.15625 to 0.15625
- routes: int32 [8192, 6], P('seq'), may hold values from 0 to 63, all different within a row; in each aligned block of 32 rows (0 to 31, 32 to 63, ...) at most 4 rows name the same one
- gate_weights: float32 [8192, 6], P('seq'), may hold values from 0.1 to 1
Outputs:
- layer_out: bfloat16 [8192, 2048], P(('seq', 'tp'))
The draws below stay inside these ranges and needn't reach their ends.
Inputs may be any that keep to these rules, and one draw needn't show every extreme that they name: `block_ids`: row d is (b, 127 - b) with b below 64; the first column names every b once. `routes`: each row names 6 different experts. In each aligned block of 32 rows (the tokens of one device) no expert is named by more than 4 rows, a bound that some block reaches.
All inputs are finite; a program needn't handle non-finite values.
Results may differ from the reference program's by a relative error of at most 0.027.
The reference program's roundings to bfloat16 on the way count: a program that leaves them out, or rounds other values in their place, can miss the bound.
Values may be sent and summed in bfloat16 or wider, within the bound.
A program may use at most 128 MiB of HBM per device.

```python
import math
import jax
import jax.numpy as jnp
import numpy as np
from jax import lax

D = 2048
HEADS = 16
NOPE = 128
ROPE = 64
LATENT = 512
VDIM = 128
FFE = 1408
TOPK = 6
TOK_DEV = 128
EXPERTS = 64
TOKENS = 8192
SUB = 32
CAP = 4
N_SEQ = 64
DEVICES = 256


def draw_block_ids(key, part):
    lower = jax.random.permutation(key, N_SEQ).astype(jnp.int32)
    return jnp.stack([lower, 2 * N_SEQ - 1 - lower], axis=1)


def draw_uk_weight(key, part):
    base_key = jax.random.fold_in(key, 7301)
    normal_key = jax.random.fold_in(base_key, 0)
    values = jnp.clip(jax.random.normal(normal_key, (HEADS, LATENT, NOPE), jnp.float32), -6.0, 6.0) * LATENT ** (-0.5)
    return values.astype(jnp.bfloat16)


def block_levels(own_key, extent, cuts, low, largest):
    def one(dim, parts):
        steps = jax.random.uniform(jax.random.fold_in(jax.random.fold_in(own_key, 6), dim), (parts,), jnp.float32, low / len(cuts), largest / len(cuts))
        return jnp.repeat(jnp.exp(steps), extent[dim] // parts).reshape((-1,) + (1,) * (len(extent) - dim - 1))

    gain = one(*cuts[0])
    for cut in cuts[1:]:
        gain = gain * one(*cut)
    return gain


def deal_out(own_key, own, number, rows, amount, top, most, lean):
    sequence = jax.random.permutation(own_key, amount)
    heavy_load, usual = load_shares(amount, rows * top, most, lean, True), load_shares(amount, rows * top, most, lean, False)
    places = jnp.arange(amount)

    def named(sizes, turn):
        used = int((sizes > 0).sum())
        fixed = max(1, used // 4)
        passed = fixed + (places - fixed + turn * (used - fixed)) % max(1, amount - fixed)
        return jnp.zeros((amount,), jnp.int32).at[sequence[jnp.where(places < fixed, places, passed)]].set(jnp.asarray(sizes, jnp.int32))

    sizes = jnp.where(number % 4 == 0, named(heavy_load, number // 4), named(usual, number - number // 4 - 1))
    mixed = jax.random.permutation(jax.random.fold_in(own, 3), amount)
    source_of, receiver = mixed[0:amount // 2 * 2:2], mixed[1:amount // 2 * 2:2]
    room = jnp.minimum(sizes[source_of] - 1, most - sizes[receiver]) // 2
    room = jnp.where((source_of == sequence[0]) | (receiver == sequence[0]) | (sizes[receiver] == 0), 0, jnp.maximum(room, 0))
    passed = jax.random.randint(jax.random.fold_in(own, 4), (amount // 2,), 0, 1 << 20) % (room + 1)
    sizes = sizes.at[source_of].add(-passed).at[receiver].add(passed)
    members = jnp.searchsorted(jnp.cumsum(sizes), jnp.arange(rows * top), side="right").astype(jnp.int32)
    grid = members.reshape(top, rows).T
    grid = grid[jax.random.permutation(jax.random.fold_in(own, 1), rows)]
    turn = jax.random.randint(jax.random.fold_in(own, 2), (rows, 1), 0, top)
    return jnp.take_along_axis(grid, (jnp.arange(top)[None, :] + turn) % top, axis=1)


def load_shares(count, total, bound, skew, full):
    loads = [(1 << 20) // math.isqrt(rank ** skew) + 1 for rank in range(1, count + 1)]
    largest = bound if full else min(bound, max(-(-total // count), total * loads[0] // sum(loads)))
    least = 1 if total - largest >= count - 1 else 0
    given, spare = [largest] + [least] * (count - 1), total - largest - least * (count - 1)
    while spare > 0:
        free = [i for i in range(1, count) if given[i] < largest] or [i for i in range(1, count) if given[i] < bound]
        whole, left = sum([loads[i] for i in free]), spare
        for i in free:
            extra = min(bound - given[i], max(1, left * loads[i] // whole), spare)
            given[i] = given[i] + extra
            spare = spare - extra
    return np.array(given)


def bell_draw(own_key, extent, width, most, cuts=(), kind=jnp.bfloat16):
    array = width * jax.random.normal(own_key, extent, jnp.float32)
    if cuts:
        array = array * block_levels(own_key, extent, cuts, -0.22, 0.18)
    return jnp.clip(array, -most, most).astype(kind)


def setup_inputs(seed: int = 0) -> dict:
    streams_of = jax.random.split(jax.random.key(seed), 16)
    tokens = bell_draw(streams_of[0], (TOKENS, D), 1.0, 6.0, ((0, 256),))
    block_ids = draw_block_ids(jax.random.fold_in(streams_of[15], 71), 0)
    attn_gain = jnp.clip(1.0 + 0.15 * jax.random.normal(streams_of[2], (D,), jnp.float32), 0.25, 1.75)
    q_weight = bell_draw(streams_of[3], (D, HEADS * (NOPE + ROPE)), D ** -0.5, 0.125, ((1, 4),))
    kv_weight = bell_draw(streams_of[4], (D, LATENT + ROPE), D ** -0.5, 0.125)
    kv_gain = jnp.clip(1.0 + 0.15 * jax.random.normal(streams_of[5], (LATENT,), jnp.float32), 0.25, 1.75)
    uk_weight = draw_uk_weight(jax.random.fold_in(streams_of[15], 71), 0)
    uv_weight = bell_draw(streams_of[7], (HEADS, LATENT, VDIM), LATENT ** -0.5, 0.25, ((0, 4),))
    o_weight = bell_draw(streams_of[8], (HEADS * VDIM, D), (HEADS * VDIM) ** -0.5, 0.125, ((0, 4),))
    ffn_gain = jnp.clip(1.0 + 0.15 * jax.random.normal(streams_of[9], (D,), jnp.float32), 0.25, 1.75)
    w_gate = bell_draw(streams_of[10], (EXPERTS, D, FFE), D ** -0.5, 0.125, ((0, 64), (2, 4)))
    w_up = bell_draw(streams_of[11], (EXPERTS, D, FFE), D ** -0.5, 0.125, ((0, 64), (2, 4)))
    w_down = bell_draw(streams_of[12], (EXPERTS, FFE, D), FFE ** -0.5, 0.15625, ((0, 64), (1, 4)))
    routes_keys = jax.random.split(jax.random.fold_in(streams_of[13], 1), TOKENS // SUB)
    routes_turns = jax.random.permutation(jax.random.fold_in(streams_of[13], 3), TOKENS // SUB)
    routes = jax.vmap(lambda own, number: deal_out(jax.random.fold_in(streams_of[13], 2), own, number, SUB, EXPERTS, TOPK, CAP, 2))(routes_keys, routes_turns).reshape((TOKENS, TOPK))
    gate_weights = jnp.clip(jnp.exp(math.log(1.0) - 2.3025851 * jax.random.uniform(streams_of[14], (TOKENS, TOPK), jnp.float32) ** block_levels(streams_of[14], (TOKENS, TOPK), ((0, 64),), -0.2, 0.2)), 0.1, 1.0)
    return {"tokens": tokens, "block_ids": block_ids, "attn_gain": attn_gain, "q_weight": q_weight, "kv_weight": kv_weight, "kv_gain": kv_gain, "uk_weight": uk_weight, "uv_weight": uv_weight, "o_weight": o_weight, "ffn_gain": ffn_gain, "w_gate": w_gate, "w_up": w_up, "w_down": w_down, "routes": routes, "gate_weights": gate_weights}


EPSILON = 1e-06

def normalize(values, gain_vec):
    values = values.astype(jnp.float32)
    factor = lax.rsqrt(lax.optimization_barrier(jnp.mean(values * values, axis=-1, keepdims=True)) + EPSILON)
    return values * factor * gain_vec

def rotate(values, position):
    half_width = values.shape[-1] // 2
    frequency = jnp.exp(jnp.arange(half_width, dtype=jnp.float32) * (-2.0 * math.log(10000.0) / values.shape[-1]))
    angles = position.astype(jnp.float32).reshape(position.shape + (1,) * (values.ndim - 1)) * frequency
    cosine = jnp.cos(angles)
    sine_part = jnp.sin(angles)
    first_half = values[..., :half_width]
    second_half = values[..., half_width:]
    return jnp.concatenate([first_half * cosine - second_half * sine_part, second_half * cosine + first_half * sine_part], axis=-1)

def positions(row_ids, block_ids, rows_dev):
    half_width = rows_dev // 2
    device = row_ids // rows_dev
    within = row_ids % rows_dev
    block_num = block_ids.reshape(-1)[device * 2 + within // half_width]
    return block_num * half_width + within % half_width

def rounded(values):
    return lax.optimization_barrier(values.astype(jnp.bfloat16)).astype(jnp.float32)

def reference(tokens, block_ids, attn_gain, q_weight, kv_weight, kv_gain, uk_weight, uv_weight, o_weight, ffn_gain, w_gate, w_up, w_down, routes, gate_weights):
    total_rows = tokens.shape[0]
    row_ids = jnp.arange(total_rows, dtype=jnp.int32)
    row_pos = positions(row_ids, block_ids, TOK_DEV)
    normed = normalize(tokens, attn_gain).astype(jnp.bfloat16)
    queries = jnp.dot(normed, q_weight, preferred_element_type=jnp.float32).astype(jnp.bfloat16)
    queries = queries.reshape(total_rows, HEADS, NOPE + ROPE)
    query_rope = rounded(rotate(queries[..., NOPE:].astype(jnp.float32), row_pos))
    query_latent = rounded(jnp.einsum('thn,hln->thl', queries[..., :NOPE].astype(jnp.float32), uk_weight.astype(jnp.float32)))
    projected = jnp.dot(normed, kv_weight, preferred_element_type=jnp.float32)
    latent = rounded(normalize(projected[:, :LATENT], kv_gain))
    key_rope = rounded(rotate(projected[:, LATENT:], row_pos))
    block_rows = math.gcd(total_rows, 256)
    score_scale = (NOPE + ROPE) ** (-0.5)

    def attend(block_index):
        first_row = block_index * block_rows
        q_lat = lax.dynamic_slice_in_dim(query_latent, first_row, block_rows, 0)
        q_rot = lax.dynamic_slice_in_dim(query_rope, first_row, block_rows, 0)
        q_pos = lax.dynamic_slice_in_dim(row_pos, first_row, block_rows, 0)
        scores = (jnp.einsum('thl,kl->thk', q_lat, latent) + jnp.einsum('thr,kr->thk', q_rot, key_rope)) * score_scale
        allowed = row_pos[None, None, :] <= q_pos[:, None, None]
        scores = jnp.where(allowed, scores, -1e+30)
        top_score = lax.optimization_barrier(jnp.max(scores, axis=-1, keepdims=True))
        exp_terms = jnp.where(allowed, jnp.exp(scores - top_score), 0.0)
        row_total = lax.optimization_barrier(jnp.sum(exp_terms, axis=-1))
        mixed_latent = jnp.einsum('thk,kl->thl', rounded(exp_terms), latent)
        return (mixed_latent / row_total[..., None]).astype(jnp.bfloat16)
    out_latent = lax.map(attend, jnp.arange(total_rows // block_rows, dtype=jnp.int32))
    out_latent = out_latent.reshape(total_rows, HEADS, LATENT)
    head_out = jnp.einsum('thl,hlv->thv', out_latent.astype(jnp.float32), uv_weight.astype(jnp.float32)).astype(jnp.bfloat16)
    head_out = head_out.reshape(total_rows, HEADS * VDIM)
    mixed = (tokens.astype(jnp.float32) + jnp.dot(head_out, o_weight, preferred_element_type=jnp.float32)).astype(jnp.bfloat16)
    normed_ffn = normalize(mixed, ffn_gain).astype(jnp.bfloat16)
    flat_routes = routes.reshape(-1)
    order_ids = jnp.argsort(flat_routes, stable=True).astype(jnp.int32)
    counts = jax.ops.segment_sum(jnp.ones_like(flat_routes), flat_routes, num_segments=EXPERTS)
    offsets = jnp.cumsum(counts) - counts
    window = DEVICES * CAP
    padded = jnp.concatenate([order_ids, jnp.zeros((window,), jnp.int32)])
    flat_gates = gate_weights.reshape(-1)

    def per_expert(accumulated, inputs):
        expert, gate_w, up_w, down_w = inputs
        picked = lax.dynamic_slice_in_dim(padded, offsets[expert].astype(jnp.int32), window, 0)
        live = jnp.arange(window, dtype=jnp.int32) < counts[expert]
        token_ids = picked // TOPK
        rows_in = normed_ffn[token_ids]
        gate_part = jnp.dot(rows_in, gate_w, preferred_element_type=jnp.float32)
        up_part = jnp.dot(rows_in, up_w, preferred_element_type=jnp.float32)
        hidden = (jax.nn.silu(gate_part) * up_part).astype(jnp.bfloat16)
        expert_out = rounded(jnp.dot(hidden, down_w, preferred_element_type=jnp.float32))
        weight_col = jnp.where(live, flat_gates[picked], 0.0)
        return (accumulated.at[token_ids].add(weight_col[:, None] * expert_out), None)
    combined, unused = lax.scan(per_expert, jnp.zeros((total_rows, D), jnp.float32), (jnp.arange(EXPERTS, dtype=jnp.int32), w_gate, w_up, w_down))
    return (mixed.astype(jnp.float32) + combined).astype(jnp.bfloat16)
```

```python
import functools
import math

import jax
import jax.numpy as jnp
from jax import lax
from jax.experimental import pallas as pl
from jax.experimental.pallas import tpu as pltpu
from jax.sharding import PartitionSpec as P

EPSILON = 1e-06
MESH = pl.DeviceIdType.MESH
BF = jnp.bfloat16
F32 = jnp.float32
KEYW = 640


def place():
    s = lax.axis_index("seq")
    t = lax.axis_index("tp")
    return (s // 32) * 4 + t, (s // 8) % 4, (s // 2) % 4, s % 2


def dev(z, y, x, c):
    z, y, x, c = z % 8, y % 4, x % 4, c % 2
    return ((z // 4) * 32 + y * 8 + x * 2 + c, z % 4)


def greet(peers):
    barrier = pltpu.get_barrier_semaphore()
    for p in peers:
        pl.semaphore_signal(barrier, inc=1, device_id=p, device_id_type=MESH)
    pl.semaphore_wait(barrier, len(peers))


def rcopy(src, dst, ss, rs, device):
    return pltpu.make_async_remote_copy(
        src_ref=src, dst_ref=dst, send_sem=ss, recv_sem=rs, device_id=device, device_id_type=MESH
    )


def normalize(values, gain_vec):
    values = values.astype(F32)
    factor = lax.rsqrt(jnp.mean(values * values, axis=-1, keepdims=True) + EPSILON)
    return values * factor * gain_vec


def rotate(values, position):
    half_width = values.shape[-1] // 2
    frequency = jnp.exp(
        jnp.arange(half_width, dtype=F32) * (-2.0 * math.log(10000.0) / values.shape[-1])
    )
    angles = position.astype(F32).reshape(position.shape + (1,) * (values.ndim - 1)) * frequency
    cosine = jnp.cos(angles)
    sine_part = jnp.sin(angles)
    first_half = values[..., :half_width]
    second_half = values[..., half_width:]
    return jnp.concatenate(
        [
            first_half * cosine - second_half * sine_part,
            second_half * cosine + first_half * sine_part,
        ],
        axis=-1,
    )


def gather_kernel(kv_ref, nt_ref, rg_ref, KV, NT, RG, ssem, rsem, lsem):
    z, y, x, c = place()
    zh, t = z // 4, z % 4
    peers = [dev(z + k, y, x, c) for k in range(1, 8)]
    xs = [dev(z, y, x + 1, c), dev(z, y, x + 3, c)]
    ys = [dev(z, y + 1, x, c), dev(z, y + 3, x, c)]
    other = dev(z, y, x, c + 1)
    greet(peers + xs + ys + [other])
    number = [0]
    sent = []

    def send(src, dst, device):
        i = number[0]
        number[0] += 1
        cp = rcopy(src, dst, ssem.at[i], rsem.at[i], device)
        cp.start()
        sent.append(cp)
        return i

    def arrived(i, region):
        rcopy(region, region, ssem.at[i], rsem.at[i], other).wait_recv()

    rows = pl.ds(pl.multiple_of(t * 32, 32), 32)
    zi = {}
    mine = KV.at[zh, y, x, c, rows]
    for k in (4, 3, 5, 2, 6, 1, 7):
        zi[k] = send(kv_ref, mine, dev(z + k, y, x, c))
    locals_ = [
        pltpu.make_async_copy(kv_ref, mine, lsem.at[0]),
        pltpu.make_async_copy(nt_ref, NT.at[t], lsem.at[1]),
        pltpu.make_async_copy(rg_ref, RG.at[zh], lsem.at[2]),
    ]
    for cp in locals_:
        cp.start()
    ri = send(rg_ref, RG.at[zh], dev(z + 4, y, x, c))
    ti = {}
    for k in (3, 2, 1):
        ti[k] = send(nt_ref, NT.at[t], (zh * 32 + y * 8 + x * 2 + c, (t + k) % 4))
    for cp in locals_:
        cp.wait()
    for k in zi:
        zz = (z - k + 8) % 8
        arrived(zi[k], KV.at[zz // 4, y, x, c, pl.ds(pl.multiple_of((zz % 4) * 32, 32), 32)])
    lo, hi = pl.ds(0, 64), pl.ds(64, 64)
    xm, xp, xo = (x + 3) % 4, (x + 1) % 4, (x + 2) % 4
    ym, yp, yo = (y + 3) % 4, (y + 1) % 4, (y + 2) % 4
    a, b = KV.at[0, y, x, c], KV.at[1, y, x, c]
    ap = send(a, a, xs[0])
    am = send(a, a, xs[1])
    bp = send(b, b, ys[0])
    bm = send(b, b, ys[1])
    arrived(ap, KV.at[0, y, xm, c])
    g = KV.at[0, y, xm, c, lo]
    ap2 = send(g, g, xs[0])
    arrived(bp, KV.at[1, ym, x, c])
    g = KV.at[1, ym, x, c, lo]
    bp2 = send(g, g, ys[0])
    arrived(am, KV.at[0, y, xp, c])
    g = KV.at[0, y, xp, c, hi]
    am2 = send(g, g, xs[1])
    arrived(bm, KV.at[1, yp, x, c])
    g = KV.at[1, yp, x, c, hi]
    bm2 = send(g, g, ys[1])
    arrived(ap2, KV.at[0, y, xo, c, lo])
    arrived(am2, KV.at[0, y, xo, c, hi])
    r = KV.at[0, y, :, c]
    rp = send(r, r, ys[0])
    rm = send(r, r, ys[1])
    arrived(bp2, KV.at[1, yo, x, c, lo])
    arrived(bm2, KV.at[1, yo, x, c, hi])
    q = KV.at[1, :, x, c]
    qp = send(q, q, xs[0])
    qm = send(q, q, xs[1])
    across = [send(r, r, other), send(q, q, other)]
    arrived(rp, KV.at[0, ym, :, c])
    g = KV.at[0, ym, :, c, lo]
    rp2 = send(g, g, ys[0])
    arrived(qp, KV.at[1, :, xm, c])
    g = KV.at[1, :, xm, c, lo]
    qp2 = send(g, g, xs[0])
    arrived(rm, KV.at[0, yp, :, c])
    g = KV.at[0, yp, :, c, hi]
    rm2 = send(g, g, ys[1])
    arrived(qm, KV.at[1, :, xp, c])
    g = KV.at[1, :, xp, c, hi]
    qm2 = send(g, g, xs[1])
    for g in (KV.at[0, ym, :, c], KV.at[1, :, xm, c], KV.at[0, yp, :, c], KV.at[1, :, xp, c]):
        across.append(send(g, g, other))
    arrived(rp2, KV.at[0, yo, :, c, lo])
    arrived(rm2, KV.at[0, yo, :, c, hi])
    g = KV.at[0, yo, :, c]
    across.append(send(g, g, other))
    arrived(qp2, KV.at[1, :, xo, c, lo])
    arrived(qm2, KV.at[1, :, xo, c, hi])
    g = KV.at[1, :, xo, c]
    across.append(send(g, g, other))
    d = 1 - c
    for i, region in zip(
        across,
        (
            KV.at[0, y, :, d],
            KV.at[1, :, x, d],
            KV.at[0, ym, :, d],
            KV.at[1, :, xm, d],
            KV.at[0, yp, :, d],
            KV.at[1, :, xp, d],
            KV.at[0, yo, :, d],
            KV.at[1, :, xo, d],
        ),
    ):
        arrived(i, region)
    for k in ti:
        arrived(ti[k], NT.at[(t - k + 4) % 4])
    arrived(ri, RG.at[1 - zh])
    for cp in sent:
        cp.wait_send()


def gather_keys(kv_own, normed_own, rg):
    count = 40
    vm = pl.BlockSpec(memory_space=pltpu.VMEM)
    return pl.pallas_call(
        gather_kernel,
        out_shape=(
            jax.ShapeDtypeStruct((2, 4, 4, 2, 128, KEYW), BF),
            jax.ShapeDtypeStruct((4, 32, 2048), BF),
            jax.ShapeDtypeStruct((2, 16, 128), F32),
        ),
        in_specs=[vm, vm, vm],
        out_specs=(pl.BlockSpec(memory_space=pl.ANY), vm, vm),
        scratch_shapes=[
            pltpu.SemaphoreType.DMA((count,)),
            pltpu.SemaphoreType.DMA((count,)),
            pltpu.SemaphoreType.DMA((3,)),
        ],
        compiler_params=pltpu.CompilerParams(
            collective_id=0, has_side_effects=True, vmem_limit_bytes=16 * 2**20
        ),
        name="gather_keys",
    )(kv_own, normed_own, rg)


CHUNK = 512


def attention_kernel(inv_ref, blk_ref, q_ref, kv_hbm, o_ref, kbuf, m_ref, l_ref, acc_ref, sems):
    low = blk_ref[0]
    per = CHUNK // 64
    top_chunks = (127 - low) // per + 1

    def fetch(p, start):
        second = p >= 64
        d = inv_ref[jnp.where(second, 127 - p, p)]
        off = pl.multiple_of(jnp.where(second, 64, 0), 64)
        cp = pltpu.make_async_copy(
            kv_hbm.at[d, pl.ds(off, 64)],
            kbuf.at[pl.ds(pl.multiple_of(p * 64, 64), 64)],
            sems.at[p // per],
        )
        cp.start()

    def issue(p, carry):
        fetch(p, True)
        return carry

    lax.fori_loop(0, top_chunks * per, issue, 0)
    scale = (128 + 64) ** (-0.5)

    for half in (1, 0):
        block = low if half == 0 else 127 - low
        last = block // per
        m_ref[...] = jnp.full_like(m_ref, -1e30)
        l_ref[...] = jnp.zeros_like(l_ref)
        acc_ref[...] = jnp.zeros_like(acc_ref)

        def step(ch, masked):
            region = kbuf.at[pl.ds(pl.multiple_of(ch * CHUNK, CHUNK), CHUNK)]
            if half == 1:
                pltpu.make_async_copy(region, region, sems.at[ch]).wait()
            keys = region[...]
            s = lax.dot_general(
                q_ref[half], keys, (((1,), (1,)), ((), ())), preferred_element_type=F32
            )
            s = s * scale
            if masked:
                row = lax.broadcasted_iota(jnp.int32, s.shape, 0) % 64
                col = lax.broadcasted_iota(jnp.int32, s.shape, 1)
                s = jnp.where(col - row <= block * 64 - ch * CHUNK, s, -1e30)
            m_old = m_ref[...]
            m_new = jnp.maximum(m_old, jnp.max(s, axis=1, keepdims=True))
            p = jnp.exp(s - m_new)
            alpha = jnp.exp(m_old - m_new)
            l_ref[...] = l_ref[...] * alpha + jnp.sum(p, axis=1, keepdims=True)
            acc_ref[...] = acc_ref[...] * alpha + jnp.dot(
                p.astype(BF), keys[:, :512], preferred_element_type=F32
            )
            m_ref[...] = m_new

        def loop(ch, carry):
            step(ch, False)
            return carry

        lax.fori_loop(0, last, loop, 0)
        step(last, True)
        o_ref[half] = (acc_ref[...] / l_ref[...]).astype(BF)


def attention(inv, low, q, kv):
    return pl.pallas_call(
        attention_kernel,
        out_shape=jax.ShapeDtypeStruct((2, 256, 512), BF),
        in_specs=[
            pl.BlockSpec(memory_space=pltpu.SMEM),
            pl.BlockSpec(memory_space=pltpu.SMEM),
            pl.BlockSpec(memory_space=pltpu.VMEM),
            pl.BlockSpec(memory_space=pl.ANY),
        ],
        out_specs=pl.BlockSpec(memory_space=pltpu.VMEM),
        scratch_shapes=[
            pltpu.VMEM((8192, KEYW), BF),
            pltpu.VMEM((256, 1), F32),
            pltpu.VMEM((256, 1), F32),
            pltpu.VMEM((256, 512), F32),
            pltpu.SemaphoreType.DMA((8192 // CHUNK,)),
        ],
        compiler_params=pltpu.CompilerParams(vmem_limit_bytes=32 * 2**20),
        name="attention",
    )(inv, low, q, kv)


def tp_scatter_kernel(p_ref, o_ref, ssem, rsem, lsem):
    z, y, x, c = place()
    s, t = lax.axis_index("seq"), lax.axis_index("tp")
    greet([(s, (t + k) % 4) for k in (1, 2, 3)])
    cps = []
    for k in (2, 3, 1):
        to = (t + k) % 4
        cp = rcopy(p_ref.at[to], o_ref.at[k], ssem.at[k], rsem.at[k], (s, to))
        cp.start()
        cps.append(cp)
    own = pltpu.make_async_copy(p_ref.at[t], o_ref.at[0], lsem)
    own.start()
    own.wait()
    for cp in cps:
        cp.wait()


def column_kernel(scatter, p_ref, o_ref, ssem, rsem, lsem):
    z, y, x, c = place()
    greet([dev(z + k, y, x, c) for k in range(1, 8)])
    cps = []
    for k in (4, 3, 5, 2, 6, 1, 7):
        to = (z + k) % 8
        if scatter:
            cp = rcopy(p_ref.at[to], o_ref.at[k], ssem.at[k], rsem.at[k], dev(to, y, x, c))
        else:
            cp = rcopy(p_ref, o_ref.at[z], ssem.at[k], rsem.at[k], dev(to, y, x, c))
        cp.start()
        cps.append(cp)
    if scatter:
        own = pltpu.make_async_copy(p_ref.at[z], o_ref.at[0], lsem)
    else:
        own = pltpu.make_async_copy(p_ref, o_ref.at[z], lsem)
    own.start()
    own.wait()
    for cp in cps:
        cp.wait()


def exchange(kernel, name, cid, array, out):
    vm = pl.BlockSpec(memory_space=pltpu.VMEM)
    return pl.pallas_call(
        kernel,
        out_shape=jax.ShapeDtypeStruct(out, BF),
        in_specs=[vm],
        out_specs=vm,
        scratch_shapes=[
            pltpu.SemaphoreType.DMA((8,)),
            pltpu.SemaphoreType.DMA((8,)),
            pltpu.SemaphoreType.DMA,
        ],
        compiler_params=pltpu.CompilerParams(
            collective_id=cid, has_side_effects=True, vmem_limit_bytes=16 * 2**20
        ),
        name=name,
    )(array)


def experts_kernel(
    sa, sb, wg, wu, wd, ra, rb, la, lb, xa, xb, oa, ob, ma, mb,
    s1, r1, s2a, r2a, s2b, r2b, s3a, r3a, s3b, r3b, s4, r4, lsem,
):
    z, y, x, c = place()
    peers = [dev(z, y, x, c + 1)]
    for k in (1, 2, 3):
        for d in (0, 1):
            peers.append(dev(z, y + k, x, c + d))
            peers.append(dev(z, y, x + k, c + d))
    greet(peers)

    def blk(j):
        return pl.ds(pl.multiple_of(j * 32, 32), 32)

    hop1a = {}
    hop1b = {}
    for k in (1, 3, 2):
        hop1a[k] = rcopy(sa.at[k], la.at[k], s1.at[k], r1.at[k], dev(z, y, x + k, c))
        hop1b[k] = rcopy(sb.at[k], lb.at[k], s1.at[4 + k], r1.at[4 + k], dev(z, y + k, x, c))
        hop1a[k].start()
        hop1b[k].start()

    def hop2a(k, src, j):
        return rcopy(
            src.at[k, blk(j)], xa.at[k, blk(j)], s2a.at[k, j], r2a.at[k, j],
            dev(z, y + j // 2, x, c + j % 2),
        )

    def hop2b(k, src, j):
        return rcopy(
            src.at[k, blk(j)], xb.at[j // 2, blk(k * 2 + j % 2)], s2b.at[k, j], r2b.at[k, j],
            dev(z, y, x + j // 2, c + j % 2),
        )

    def own2(k, sra, srb):
        return (
            pltpu.make_async_copy(sra.at[k, blk(0)], xa.at[k, blk(0)], lsem.at[k]),
            pltpu.make_async_copy(srb.at[k, blk(0)], xb.at[0, blk(k * 2)], lsem.at[4 + k]),
        )

    for k in (0, 1, 3, 2):
        if k:
            hop1a[k].wait_recv()
            hop1b[k].wait_recv()
        sra, srb = (la, lb) if k else (sa, sb)
        for j in (2, 6, 4, 3, 7, 5, 1):
            hop2a(k, sra, j).start()
            hop2b(k, srb, j).start()
        for cp in own2(k, sra, srb):
            cp.start()
    for k in range(4):
        sra, srb = (la, lb) if k else (sa, sb)
        for cp in own2(k, sra, srb):
            cp.wait()

    def hop3a(k, j, dst):
        return rcopy(
            oa.at[k, blk(j)], dst.at[k, blk(j)], s3a.at[k, j], r3a.at[k, j],
            dev(z, y + 4 - j // 2, x, c + j % 2),
        )

    def hop3b(k, j, dst):
        return rcopy(
            ob.at[k, blk(j)], dst.at[j // 2, blk(k * 2 + j % 2)], s3b.at[k, j], r3b.at[k, j],
            dev(z, y, x + 4 - k, c + j % 2),
        )

    def own3(k):
        return ()

    for k in (0, 1, 3, 2):
        for j in range(1, 8):
            hop2a(k, la, j).wait_recv()
        for i in range(4):
            for d in (0, 1):
                if k or d:
                    hop2b(i, lb, k * 2 + d).wait_recv()
        rows_a = xa[k]
        rows_b = xb[k]
        gate = jnp.dot(rows_a, wg[:1024], preferred_element_type=F32) + jnp.dot(
            rows_b, wg[1024:], preferred_element_type=F32
        )
        up = jnp.dot(rows_a, wu[:1024], preferred_element_type=F32) + jnp.dot(
            rows_b, wu[1024:], preferred_element_type=F32
        )
        hidden = (gate / (1.0 + jnp.exp(-gate)) * up).astype(BF)
        oa[k] = jnp.dot(hidden, wd[:, :1024], preferred_element_type=F32).astype(BF)
        ob[k] = jnp.dot(hidden, wd[:, 1024:], preferred_element_type=F32).astype(BF)
        for j in range(1, 8):
            hop3a(k, j, ma if k else ra).start()
        cp = pltpu.make_async_copy(
            oa.at[k, blk(0)], (ma if k else ra).at[k, blk(0)], lsem.at[8 + k]
        )
        cp.start()
        for j in range(8):
            i = j // 2
            if k or j % 2:
                hop3b(k, j, mb if i else rb).start()
            else:
                pltpu.make_async_copy(
                    ob.at[k, blk(j)], (mb if i else rb).at[i, blk(0)], lsem.at[12 + i]
                ).start()

    hop4 = []
    for k in (1, 3, 2):
        for j in range(1, 8):
            hop3a(k, j, ma).wait_recv()
        pltpu.make_async_copy(oa.at[k, blk(0)], ma.at[k, blk(0)], lsem.at[8 + k]).wait()
        cp = rcopy(ma.at[k], ra.at[k], s4.at[k], r4.at[k], dev(z, y, x + 4 - k, c))
        cp.start()
        hop4.append(cp)
    for i in (1, 3, 2):
        for k in range(4):
            for d in (0, 1):
                if k or d:
                    hop3b(k, i * 2 + d, mb).wait_recv()
        pltpu.make_async_copy(ob.at[0, blk(i * 2)], mb.at[i, blk(0)], lsem.at[12 + i]).wait()
        cp = rcopy(mb.at[i], rb.at[i], s4.at[4 + i], r4.at[4 + i], dev(z, y + 4 - i, x, c))
        cp.start()
        hop4.append(cp)
    for j in range(1, 8):
        hop3a(0, j, ra).wait_recv()
    pltpu.make_async_copy(oa.at[0, blk(0)], ra.at[0, blk(0)], lsem.at[8]).wait()
    for k in range(4):
        for d in (0, 1):
            if k or d:
                hop3b(k, d, rb).wait_recv()
    pltpu.make_async_copy(ob.at[0, blk(0)], rb.at[0, blk(0)], lsem.at[12]).wait()
    for cp in hop4:
        cp.wait()
    for k in (1, 2, 3):
        hop1a[k].wait_send()
        hop1b[k].wait_send()
    for k in range(4):
        for j in range(1, 8):
            hop2a(k, la, j).wait_send()
            hop2b(k, lb, j).wait_send()
            hop3a(k, j, ma).wait_send()
        for j in range(8):
            if k or j % 2:
                hop3b(k, j, mb).wait_send()


def experts(sa, sb, wg, wu, wd):
    vm = pl.BlockSpec(memory_space=pltpu.VMEM)
    big = (4, 256, 1024)
    dma = pltpu.SemaphoreType.DMA
    return pl.pallas_call(
        experts_kernel,
        out_shape=(jax.ShapeDtypeStruct(big, BF), jax.ShapeDtypeStruct(big, BF)),
        in_specs=[vm] * 5,
        out_specs=(vm, vm),
        scratch_shapes=[pltpu.VMEM(big, BF)] * 8
        + [
            dma((8,)), dma((8,)),
            dma((4, 8)), dma((4, 8)), dma((4, 8)), dma((4, 8)),
            dma((4, 8)), dma((4, 8)), dma((4, 8)), dma((4, 8)),
            dma((8,)), dma((8,)),
            dma((16,)),
        ],
        compiler_params=pltpu.CompilerParams(
            collective_id=4, has_side_effects=True, vmem_limit_bytes=56 * 2**20
        ),
        name="experts",
    )(sa, sb, wg, wu, wd)


def slot_tables(routes, gates, z, y, x, c):
    e_dy = lax.broadcasted_iota(jnp.int32, (4, 4, 2), 0)
    e_dx = lax.broadcasted_iota(jnp.int32, (4, 4, 2), 1)
    e_dc = lax.broadcasted_iota(jnp.int32, (4, 4, 2), 2)
    expert = (z // 4) * 32 + ((y + e_dy) % 4) * 8 + ((x + e_dx) % 4) * 2 + (c + e_dc) % 2
    expert = expert.reshape(32)
    hit = routes[:, :, None] == expert[None, None, :]
    member = jnp.any(hit, axis=1)
    gate = jnp.sum(jnp.where(hit, gates[:, :, None], 0.0), axis=1)
    ti = lax.broadcasted_iota(jnp.int32, (256, 256), 0)
    tj = lax.broadcasted_iota(jnp.int32, (256, 256), 1)
    before = ((tj < ti) & (tj // 32 == ti // 32)).astype(BF)
    rank = jnp.dot(before, member.astype(BF), preferred_element_type=F32).astype(jnp.int32)
    token = lax.broadcasted_iota(jnp.int32, (256, 32), 0)
    slot = jnp.where(member, (token // 32) * 4 + rank, -1)
    number = lax.broadcasted_iota(jnp.int32, (32, 32, 256), 1)
    pick = slot.T[:, None, :] == number
    table_b = pick.astype(BF)
    weighted = jnp.where(pick, gate.T[:, None, :], 0.0)
    hi = weighted.astype(BF)
    lo = (weighted - hi.astype(F32)).astype(BF)

    def swap(v):
        return v.reshape(4, 4, 2, 32, 256).transpose(1, 0, 2, 3, 4).reshape(1024, 256)

    flat = lambda v: v.reshape(1024, 256)
    return (swap(table_b), flat(table_b)), ((swap(hi), swap(lo)), (flat(hi), flat(lo)))


def body(
    tokens, block_ids, attn_gain, q_weight, kv_weight, kv_gain, uk_weight, uv_weight,
    o_weight, ffn_gain, w_gate, w_up, w_down, routes, gate_weights,
):
    z, y, x, c = place()
    t = lax.axis_index("tp")
    s = lax.axis_index("seq")
    own_blocks = lax.dynamic_slice(block_ids, (s, 0), (1, 2))[0]
    normed_own = normalize(tokens, attn_gain).astype(BF)
    own_pos = own_blocks[t // 2] * 64 + (t % 2) * 32 + jnp.arange(32, dtype=jnp.int32)
    projected = jnp.dot(normed_own, kv_weight, preferred_element_type=F32)
    latent = normalize(projected[:, :512], kv_gain).astype(BF)
    key_rope = rotate(projected[:, 512:], own_pos).astype(BF)
    kv_own = jnp.concatenate([latent, key_rope, jnp.zeros((32, 64), BF)], axis=1)
    pad2 = jnp.zeros((2, 128), F32)
    rg = jnp.concatenate([routes.astype(F32).T, pad2, gate_weights.T, pad2], axis=0)
    kv, normed, rgs = gather_keys(kv_own, normed_own, rg)

    normed = normed.reshape(128, 2048)
    query_pos = (own_blocks[:, None] * 64 + jnp.arange(64, dtype=jnp.int32)[None, :]).reshape(128)
    queries = jnp.dot(normed, q_weight, preferred_element_type=F32).astype(BF)
    queries = queries.reshape(128, 4, 192)
    query_rope = rotate(queries[..., 128:].astype(F32), query_pos).astype(BF)
    query_latent = jnp.einsum(
        "thn,hln->htl", queries[..., :128], uk_weight, preferred_element_type=F32
    ).astype(BF)
    q = jnp.concatenate(
        [query_latent, query_rope.transpose(1, 0, 2), jnp.zeros((4, 128, 64), BF)], axis=2
    )
    q = q.reshape(4, 2, 64, KEYW).transpose(1, 0, 2, 3).reshape(2, 256, KEYW)
    ids = jnp.arange(64, dtype=jnp.int32)
    inv = jnp.sum(
        jnp.where(block_ids[:, 0][None, :] == ids[:, None], ids[None, :], 0), axis=1
    ).astype(jnp.int32)
    out_latent = attention(inv, own_blocks[:1], q, kv.reshape(64, 128, KEYW))
    out_latent = out_latent.reshape(2, 4, 64, 512).transpose(1, 0, 2, 3).reshape(4, 128, 512)
    head_out = jnp.einsum(
        "htl,hlv->thv", out_latent, uv_weight, preferred_element_type=F32
    ).astype(BF)
    partial_out = jnp.dot(head_out.reshape(128, 512), o_weight, preferred_element_type=F32)
    parts = exchange(
        tp_scatter_kernel, "tp_scatter", 1, partial_out.astype(BF).reshape(4, 32, 2048),
        (4, 32, 2048),
    )
    attn_own = jnp.sum(parts.astype(F32), axis=0)
    mixed = (tokens.astype(F32) + attn_own).astype(BF)
    normed_ffn = normalize(mixed, ffn_gain).astype(BF)
    column = exchange(
        functools.partial(column_kernel, False), "column_gather", 2, normed_ffn, (8, 32, 2048)
    ).reshape(256, 2048)

    all_routes = rgs[:, :6].transpose(0, 2, 1).reshape(256, 6).astype(jnp.int32)
    all_gates = rgs[:, 8:14].transpose(0, 2, 1).reshape(256, 6)
    (pa, pb), (ca, cb) = slot_tables(all_routes, all_gates, z, y, x, c)
    sa = jnp.dot(pa, column[:, :1024], preferred_element_type=F32).astype(BF)
    sb = jnp.dot(pb, column[:, 1024:], preferred_element_type=F32).astype(BF)
    ra, rb = experts(
        sa.reshape(4, 256, 1024), sb.reshape(4, 256, 1024), w_gate[0], w_up[0], w_down[0]
    )

    def combine(tables, returned):
        returned = returned.reshape(1024, 1024)
        hi, lo = tables
        dims = (((0,), (0,)), ((), ()))
        return lax.dot_general(hi, returned, dims, preferred_element_type=F32) + lax.dot_general(
            lo, returned, dims, preferred_element_type=F32
        )

    combined = jnp.concatenate([combine(ca, ra), combine(cb, rb)], axis=1).astype(BF)
    sums = exchange(
        functools.partial(column_kernel, True), "column_scatter", 3,
        combined.reshape(8, 32, 2048), (8, 32, 2048),
    )
    return (mixed.astype(F32) + jnp.sum(sums.astype(F32), axis=0)).astype(BF)


def solution(mesh):
    return jax.shard_map(
        body,
        mesh=mesh,
        in_specs=(
            P(("seq", "tp"), None), P(), P(), P(None, "tp"), P(), P(),
            P("tp", None, None), P("tp", None, None), P("tp", None), P(),
            P("seq", None, "tp"), P("seq", None, "tp"), P("seq", "tp", None),
            P("seq", None), P("seq", None),
        ),
        out_specs=P(("seq", "tp"), None),
        check_vma=False,
    )
```

```python
import functools
import math

import jax
import jax.numpy as jnp
from jax import lax
from jax.experimental import pallas as pl
from jax.experimental.pallas import tpu as pltpu
from jax.sharding import PartitionSpec as P

EPSILON = 1e-06
MESH = pl.DeviceIdType.MESH
BF = jnp.bfloat16
F32 = jnp.float32
KEYW = 640


def place():
    s = lax.axis_index("seq")
    t = lax.axis_index("tp")
    return (s // 32) * 4 + t, (s // 8) % 4, (s // 2) % 4, s % 2


def dev(z, y, x, c):
    z, y, x, c = z % 8, y % 4, x % 4, c % 2
    return ((z // 4) * 32 + y * 8 + x * 2 + c, z % 4)


def greet(peers):
    barrier = pltpu.get_barrier_semaphore()
    for p in peers:
        pl.semaphore_signal(barrier, inc=1, device_id=p, device_id_type=MESH)
    pl.semaphore_wait(barrier, len(peers))


def rcopy(src, dst, ss, rs, device):
    return pltpu.make_async_remote_copy(
        src_ref=src, dst_ref=dst, send_sem=ss, recv_sem=rs, device_id=device, device_id_type=MESH
    )


def normalize(values, gain_vec):
    values = values.astype(F32)
    factor = lax.rsqrt(jnp.mean(values * values, axis=-1, keepdims=True) + EPSILON)
    return values * factor * gain_vec


def rotate(values, position):
    half_width = values.shape[-1] // 2
    frequency = jnp.exp(
        jnp.arange(half_width, dtype=F32) * (-2.0 * math.log(10000.0) / values.shape[-1])
    )
    angles = position.astype(F32).reshape(position.shape + (1,) * (values.ndim - 1)) * frequency
    cosine = jnp.cos(angles)
    sine_part = jnp.sin(angles)
    first_half = values[..., :half_width]
    second_half = values[..., half_width:]
    return jnp.concatenate(
        [
            first_half * cosine - second_half * sine_part,
            second_half * cosine + first_half * sine_part,
        ],
        axis=-1,
    )


def gather_kernel(kv_ref, nt_ref, rg_ref, KV, NT, RG, ssem, rsem, lsem):
    z, y, x, c = place()
    zh, t = z // 4, z % 4
    peers = [dev(z + k, y, x, c) for k in range(1, 8)]
    xs = [dev(z, y, x + 1, c), dev(z, y, x + 3, c), dev(z, y, x + 2, c)]
    ys = [dev(z, y + 1, x, c), dev(z, y + 3, x, c), dev(z, y + 2, x, c)]
    other = dev(z, y, x, c + 1)
    greet(peers + xs + ys + [other])
    number = [0]
    sent = []

    def send(src, dst, device):
        i = number[0]
        number[0] += 1
        cp = rcopy(src, dst, ssem.at[i], rsem.at[i], device)
        cp.start()
        sent.append(cp)
        return i

    def arrived(i, region):
        rcopy(region, region, ssem.at[i], rsem.at[i], other).wait_recv()

    rows = pl.ds(pl.multiple_of(t * 32, 32), 32)
    zi = {}
    mine = KV.at[zh, y, x, c, rows]
    for k in (4, 3, 5, 2, 6, 1, 7):
        zi[k] = send(kv_ref, mine, dev(z + k, y, x, c))
    locals_ = [
        pltpu.make_async_copy(kv_ref, mine, lsem.at[0]),
        pltpu.make_async_copy(nt_ref, NT.at[t], lsem.at[1]),
        pltpu.make_async_copy(rg_ref, RG.at[0, 0, zh], lsem.at[2]),
    ]
    for cp in locals_:
        cp.start()
    ri = send(rg_ref, RG.at[0, 0, zh], dev(z + 4, y, x, c))
    ti = {}
    for k in (3, 2, 1):
        ti[k] = send(nt_ref, NT.at[t], (zh * 32 + y * 8 + x * 2 + c, (t + k) % 4))
    for cp in locals_:
        cp.wait()
    for k in zi:
        zz = (z - k + 8) % 8
        arrived(zi[k], KV.at[zz // 4, y, x, c, pl.ds(pl.multiple_of((zz % 4) * 32, 32), 32)])
    arrived(ri, RG.at[0, 0, 1 - zh])
    spare = pltpu.make_async_copy(RG.at[0, 0], RG.at[1, 0], lsem.at[2])
    spare.start()
    routes_sent = []
    for k in (1, 2, 3):
        g = RG.at[0, 0]
        routes_sent.append((send(g, RG.at[0, k], dev(z, y, x + k, c)), RG.at[0, k]))
        routes_sent.append((send(g, RG.at[1, k], dev(z, y + k, x, c)), RG.at[1, k]))
    lo, hi = pl.ds(0, 64), pl.ds(64, 64)
    xm, xp, xo = (x + 3) % 4, (x + 1) % 4, (x + 2) % 4
    ym, yp, yo = (y + 3) % 4, (y + 1) % 4, (y + 2) % 4
    a, b = KV.at[0, y, x, c], KV.at[1, y, x, c]
    ap = send(a, a, xs[0])
    am = send(a, a, xs[1])
    bp = send(b, b, ys[0])
    bm = send(b, b, ys[1])
    arrived(ap, KV.at[0, y, xm, c])
    g = KV.at[0, y, xm, c, lo]
    ap2 = send(g, g, xs[0])
    arrived(bp, KV.at[1, ym, x, c])
    g = KV.at[1, ym, x, c, lo]
    bp2 = send(g, g, ys[0])
    arrived(am, KV.at[0, y, xp, c])
    g = KV.at[0, y, xp, c, hi]
    am2 = send(g, g, xs[1])
    arrived(bm, KV.at[1, yp, x, c])
    g = KV.at[1, yp, x, c, hi]
    bm2 = send(g, g, ys[1])
    arrived(ap2, KV.at[0, y, xo, c, lo])
    arrived(am2, KV.at[0, y, xo, c, hi])
    r = KV.at[0, y, :, c]
    rp = send(r, r, ys[0])
    rm = send(r, r, ys[1])
    arrived(bp2, KV.at[1, yo, x, c, lo])
    arrived(bm2, KV.at[1, yo, x, c, hi])
    q = KV.at[1, :, x, c]
    qp = send(q, q, xs[0])
    qm = send(q, q, xs[1])
    across = [send(r, r, other), send(q, q, other)]
    arrived(rp, KV.at[0, ym, :, c])
    g = KV.at[0, ym, :, c, lo]
    rp2 = send(g, g, ys[0])
    arrived(qp, KV.at[1, :, xm, c])
    g = KV.at[1, :, xm, c, lo]
    qp2 = send(g, g, xs[0])
    arrived(rm, KV.at[0, yp, :, c])
    g = KV.at[0, yp, :, c, hi]
    rm2 = send(g, g, ys[1])
    arrived(qm, KV.at[1, :, xp, c])
    g = KV.at[1, :, xp, c, hi]
    qm2 = send(g, g, xs[1])
    for g in (KV.at[0, ym, :, c], KV.at[1, :, xm, c], KV.at[0, yp, :, c], KV.at[1, :, xp, c]):
        across.append(send(g, g, other))
    arrived(rp2, KV.at[0, yo, :, c, lo])
    arrived(rm2, KV.at[0, yo, :, c, hi])
    g = KV.at[0, yo, :, c]
    across.append(send(g, g, other))
    arrived(qp2, KV.at[1, :, xo, c, lo])
    arrived(qm2, KV.at[1, :, xo, c, hi])
    g = KV.at[1, :, xo, c]
    across.append(send(g, g, other))
    d = 1 - c
    for i, region in zip(
        across,
        (
            KV.at[0, y, :, d],
            KV.at[1, :, x, d],
            KV.at[0, ym, :, d],
            KV.at[1, :, xm, d],
            KV.at[0, yp, :, d],
            KV.at[1, :, xp, d],
            KV.at[0, yo, :, d],
            KV.at[1, :, xo, d],
        ),
    ):
        arrived(i, region)
    for k in ti:
        arrived(ti[k], NT.at[(t - k + 4) % 4])
    spare.wait()
    for i, region in routes_sent:
        arrived(i, region)
    for cp in sent:
        cp.wait_send()


def gather_keys(kv_own, normed_own, rg):
    count = 48
    vm = pl.BlockSpec(memory_space=pltpu.VMEM)
    return pl.pallas_call(
        gather_kernel,
        out_shape=(
            jax.ShapeDtypeStruct((2, 4, 4, 2, 128, KEYW), BF),
            jax.ShapeDtypeStruct((4, 32, 2048), BF),
            jax.ShapeDtypeStruct((2, 4, 2, 16, 128), F32),
        ),
        in_specs=[vm, vm, vm],
        out_specs=(pl.BlockSpec(memory_space=pltpu.HBM), vm, vm),
        scratch_shapes=[
            pltpu.SemaphoreType.DMA((count,)),
            pltpu.SemaphoreType.DMA((count,)),
            pltpu.SemaphoreType.DMA((3,)),
        ],
        compiler_params=pltpu.CompilerParams(
            collective_id=0, has_side_effects=True, vmem_limit_bytes=16 * 2**20
        ),
        name="gather_keys",
    )(kv_own, normed_own, rg)


CHUNK = 1024


def attention_kernel(inv_ref, blk_ref, q_ref, kv_hbm, o_ref, kbuf, m_ref, l_ref, acc_ref, sems):
    low = blk_ref[0]
    per = CHUNK // 64
    top_chunks = (127 - low) // per + 1

    def issue(p, carry):
        second = p >= 64
        d = inv_ref[jnp.where(second, 127 - p, p)]
        off = pl.multiple_of(jnp.where(second, 64, 0), 64)
        pltpu.make_async_copy(
            kv_hbm.at[d, pl.ds(off, 64)],
            kbuf.at[pl.ds(pl.multiple_of(p * 64, 64), 64)],
            sems.at[p // per],
        ).start()
        return carry

    lax.fori_loop(0, top_chunks * per, issue, 0)
    scale = (128 + 64) ** (-0.5)

    for half in (1, 0):
        block = low if half == 0 else 127 - low
        last = block // per
        m_ref[...] = jnp.full_like(m_ref, -1e30)
        l_ref[...] = jnp.zeros_like(l_ref)
        acc_ref[...] = jnp.zeros_like(acc_ref)

        def step(ch, masked):
            region = kbuf.at[pl.ds(pl.multiple_of(ch * CHUNK, CHUNK), CHUNK)]
            if half == 1:
                pltpu.make_async_copy(region, region, sems.at[ch]).wait()
            keys = region[...]
            s = jnp.dot(keys, q_ref[half], preferred_element_type=F32) * scale
            if masked:
                key = lax.broadcasted_iota(jnp.int32, s.shape, 0)
                query = lax.broadcasted_iota(jnp.int32, s.shape, 1) % 64
                s = jnp.where(key - query <= block * 64 - ch * CHUNK, s, -1e30)
            m_old = m_ref[...]
            m_new = jnp.maximum(m_old, jnp.max(s, axis=0, keepdims=True))
            p = jnp.exp(s - m_new)
            alpha = jnp.exp(m_old - m_new)
            l_ref[...] = l_ref[...] * alpha + jnp.sum(p, axis=0, keepdims=True)
            m_ref[...] = m_new
            acc_ref[...] = acc_ref[...] * alpha + lax.dot_general(
                keys[:, :512], p.astype(BF), (((0,), (0,)), ((), ())), preferred_element_type=F32
            )

        def loop(ch, carry):
            step(ch, False)
            return carry

        lax.fori_loop(0, last, loop, 0)
        step(last, True)
        o_ref[half] = (acc_ref[...] / l_ref[...]).T.astype(BF)


def attention(inv, low, q, kv):
    return pl.pallas_call(
        attention_kernel,
        out_shape=jax.ShapeDtypeStruct((2, 256, 512), BF),
        in_specs=[
            pl.BlockSpec(memory_space=pltpu.SMEM),
            pl.BlockSpec(memory_space=pltpu.SMEM),
            pl.BlockSpec(memory_space=pltpu.VMEM),
            pl.BlockSpec(memory_space=pltpu.HBM),
        ],
        out_specs=pl.BlockSpec(memory_space=pltpu.VMEM),
        scratch_shapes=[
            pltpu.VMEM((8192, KEYW), BF),
            pltpu.VMEM((1, 256), F32),
            pltpu.VMEM((1, 256), F32),
            pltpu.VMEM((512, 256), F32),
            pltpu.SemaphoreType.DMA((8192 // CHUNK,)),
        ],
        compiler_params=pltpu.CompilerParams(vmem_limit_bytes=32 * 2**20),
        name="attention",
    )(inv, low, q, kv)


def tp_scatter_kernel(p_ref, o_ref, ssem, rsem, lsem):
    z, y, x, c = place()
    s, t = lax.axis_index("seq"), lax.axis_index("tp")
    greet([(s, (t + k) % 4) for k in (1, 2, 3)])
    cps = []
    for k in (2, 3, 1):
        to = (t + k) % 4
        cp = rcopy(p_ref.at[to], o_ref.at[k], ssem.at[k], rsem.at[k], (s, to))
        cp.start()
        cps.append(cp)
    own = pltpu.make_async_copy(p_ref.at[t], o_ref.at[0], lsem)
    own.start()
    own.wait()
    for cp in cps:
        cp.wait()


def column_gather_kernel(p_ref, o_ref, ssem, rsem, lsem):
    z, y, x, c = place()
    towards = (dev(z + 1, y, x, c), dev(z + 7, y, x, c))
    greet(towards)

    def shard(d, s):
        return (z + 8 - s) % 8 if d == 0 else (z + s) % 8

    def hop(d, s, h):
        rows = pl.ds(h * 16, 16)
        src = p_ref.at[rows] if s == 1 else o_ref.at[shard(d, s - 1), rows]
        return rcopy(
            src, o_ref.at[shard(d, s - 1), rows], ssem.at[d, s - 1, h], rsem.at[d, s - 1, h],
            towards[d],
        )

    def arrived(d, s, h):
        region = o_ref.at[shard(d, s), pl.ds(h * 16, 16)]
        rcopy(region, region, ssem.at[d, s - 1, h], rsem.at[d, s - 1, h], towards[d]).wait_recv()

    for h in (0, 1):
        for d in (0, 1):
            hop(d, 1, h).start()
    own = pltpu.make_async_copy(p_ref, o_ref.at[z], lsem)
    own.start()
    for s in (2, 3, 4):
        for h in (0, 1):
            for d in (0, 1):
                arrived(d, s - 1, h)
                if s < 4 or h == d:
                    hop(d, s, h).start()
    own.wait()
    for d in (0, 1):
        arrived(d, 4, d)
        for s in (1, 2, 3):
            for h in (0, 1):
                hop(d, s, h).wait_send()
        hop(d, 4, d).wait_send()


def column_gather(array):
    vm = pl.BlockSpec(memory_space=pltpu.VMEM)
    return pl.pallas_call(
        column_gather_kernel,
        out_shape=jax.ShapeDtypeStruct((8, 32, 2048), BF),
        in_specs=[vm],
        out_specs=vm,
        scratch_shapes=[
            pltpu.SemaphoreType.DMA((2, 4, 2)),
            pltpu.SemaphoreType.DMA((2, 4, 2)),
            pltpu.SemaphoreType.DMA,
        ],
        compiler_params=pltpu.CompilerParams(
            collective_id=2, has_side_effects=True, vmem_limit_bytes=16 * 2**20
        ),
        name="column_gather",
    )(array)


def column_scatter_kernel(p_ref, o_ref, rbuf, sbuf, ssem, rsem):
    z, y, x, c = place()
    towards = (dev(z + 1, y, x, c), dev(z + 7, y, x, c))
    greet(towards)

    def target(d, s):
        return (z + 5 - s) % 8 if d == 0 else (z + 3 + s) % 8

    def hop(d, s, h, src):
        rows = pl.ds(h * 16, 16)
        return rcopy(
            src.at[rows], rbuf.at[d, s - 1, rows], ssem.at[d, s - 1, h], rsem.at[d, s - 1, h],
            towards[d],
        )

    started = []
    for d in (0, 1):
        cp = hop(d, 1, d, p_ref.at[target(d, 1)])
        cp.start()
        started.append(cp)
    for d in (0, 1):
        cp = hop(d, 2, 1 - d, p_ref.at[target(d, 2)])
        cp.start()
        started.append(cp)
    for s in (2, 3, 4):
        for h in (0, 1):
            todo = []
            for d in (0, 1):
                if s == 2 and h != d:
                    continue
                rows = pl.ds(h * 16, 16)
                hop(d, s - 1, h, sbuf.at[d, s - 1]).wait_recv()
                sbuf[d, s - 1, rows] = (
                    p_ref[target(d, s), rows].astype(F32) + rbuf[d, s - 2, rows].astype(F32)
                ).astype(BF)
                todo.append(hop(d, s, h, sbuf.at[d, s - 1]))
            for cp in todo:
                cp.start()
                started.append(cp)
    for h in (0, 1):
        for d in (0, 1):
            hop(d, 4, h, sbuf.at[d, 3]).wait_recv()
    o_ref[...] = (
        p_ref[z].astype(F32) + rbuf[0, 3].astype(F32) + rbuf[1, 3].astype(F32)
    )
    for cp in started:
        cp.wait_send()


def column_scatter(array):
    vm = pl.BlockSpec(memory_space=pltpu.VMEM)
    return pl.pallas_call(
        column_scatter_kernel,
        out_shape=jax.ShapeDtypeStruct((32, 2048), F32),
        in_specs=[vm],
        out_specs=vm,
        scratch_shapes=[
            pltpu.VMEM((2, 4, 32, 2048), BF),
            pltpu.VMEM((2, 4, 32, 2048), BF),
            pltpu.SemaphoreType.DMA((2, 4, 2)),
            pltpu.SemaphoreType.DMA((2, 4, 2)),
        ],
        compiler_params=pltpu.CompilerParams(
            collective_id=3, has_side_effects=True, vmem_limit_bytes=16 * 2**20
        ),
        name="column_scatter",
    )(array)


def exchange(kernel, name, cid, array, out):
    vm = pl.BlockSpec(memory_space=pltpu.VMEM)
    return pl.pallas_call(
        kernel,
        out_shape=jax.ShapeDtypeStruct(out, BF),
        in_specs=[vm],
        out_specs=vm,
        scratch_shapes=[
            pltpu.SemaphoreType.DMA((8,)),
            pltpu.SemaphoreType.DMA((8,)),
            pltpu.SemaphoreType.DMA,
        ],
        compiler_params=pltpu.CompilerParams(
            collective_id=cid, has_side_effects=True, vmem_limit_bytes=16 * 2**20
        ),
        name=name,
    )(array)


def turn(i):
    return ((i * (i + 1)) // 2) % 4


def experts_kernel(
    xin, sla, slb, gta, gtb, wg, wu, wd, out,
    ta, tb, sa, sb, ra, rb, oa, ob, ma, mb, pa, pb, qa, qb,
    s1, r1, s2a, r2a, s2b, r2b, s3a, r3a, s3b, r3b, s4, r4, lsem,
):
    z, y, x, c = place()
    peers = [dev(z, y, x, c + 1)]
    for k in (1, 2, 3):
        for d in (0, 1):
            peers.append(dev(z, y + k, x, c + d))
            peers.append(dev(z, y, x + k, c + d))
    greet(peers)
    left, right = pl.ds(0, 1024), pl.ds(1024, 1024)
    low, high = pl.ds(0, 128), pl.ds(128, 128)

    def blk(j):
        return pl.ds(pl.multiple_of(j * 32, 32), 32)

    def where_x(k):
        return dev(z, y, x + k, c)

    def where_y(k):
        return dev(z, y + k, x, c)

    def first(k):
        return (
            rcopy(xin.at[:, left], ta.at[k], s1.at[0, k], r1.at[0, k], where_x(k)),
            rcopy(xin.at[:, right], tb.at[k], s1.at[1, k], r1.at[1, k], where_y(k)),
        )

    def onward(k):
        rows, i = (low, 2) if k == 1 else (high, 0)
        return (
            rcopy(ta.at[k, rows], ta.at[2, rows], s1.at[0, i], r1.at[0, i], where_x(k)),
            rcopy(tb.at[k, rows], tb.at[2, rows], s1.at[1, i], r1.at[1, i], where_y(k)),
        )

    for k in (1, 3):
        for cp in first(k):
            cp.start()
    ta[0] = xin[:, :1024]
    tb[0] = xin[:, 1024:]

    def hop2a(k, j):
        return rcopy(
            sa.at[k, blk(j)], ra.at[k, blk(j)], s2a.at[k, j], r2a.at[k, j],
            dev(z, y + j // 2, x, c + j % 2),
        )

    def hop2b(k, j):
        return rcopy(
            sb.at[k, blk(j)], rb.at[j // 2, blk(k * 2 + j % 2)], s2b.at[k, j], r2b.at[k, j],
            dev(z, y, x + j // 2, c + j % 2),
        )

    def own2(k):
        return (
            pltpu.make_async_copy(sa.at[k, blk(0)], ra.at[k, blk(0)], lsem.at[k]),
            pltpu.make_async_copy(sb.at[k, blk(0)], rb.at[0, blk(k * 2)], lsem.at[4 + k]),
        )

    number = lax.broadcasted_iota(jnp.int32, (8, 32, 256), 1).astype(F32)

    def table(slots, k):
        return (slots[k][:, None, :] == number).astype(F32)

    def spread(i, carry):
        k = turn(i)

        @pl.when(i == 1)
        def _():
            for n in (1, 3):
                for cp, cp2 in zip(first(n), onward(n)):
                    cp.wait_recv()
                    cp2.start()

        @pl.when(i == 3)
        def _():
            for n in (1, 3):
                for cp in onward(n):
                    cp.wait_recv()

        sa[k] = jnp.dot(
            table(sla, k).reshape(256, 256).astype(BF), ta[k], preferred_element_type=F32
        ).astype(BF)
        sb[k] = jnp.dot(
            table(slb, k).reshape(256, 256).astype(BF), tb[k], preferred_element_type=F32
        ).astype(BF)
        for j in (2, 6, 4, 3, 7, 5, 1):
            hop2a(k, j).start()
            hop2b(k, j).start()
        for cp in own2(k):
            cp.start()
        return carry

    lax.fori_loop(0, 4, spread, 0)

    def hop3a(k, j):
        return rcopy(
            oa.at[k, blk(j)], ma.at[k, blk(j)], s3a.at[k, j], r3a.at[k, j],
            dev(z, y + 4 - j // 2, x, c + j % 2),
        )

    def hop3b(k, j):
        return rcopy(
            ob.at[k, blk(j)], mb.at[j // 2, blk(k * 2 + j % 2)], s3b.at[k, j], r3b.at[k, j],
            dev(z, y, x + 4 - k, c + j % 2),
        )

    def own3(k):
        return (
            pltpu.make_async_copy(oa.at[k, blk(0)], ma.at[k, blk(0)], lsem.at[8 + k]),
            pltpu.make_async_copy(ob.at[0, blk(k * 2)], mb.at[k, blk(0)], lsem.at[12 + k]),
        )

    for k in range(4):
        for cp in own2(k):
            cp.wait()

    def across(rows, weight):
        return lax.dot_general(
            rows, weight, (((1,), (1,)), ((), ())), preferred_element_type=F32
        )

    def work(i, carry):
        k = turn(i)
        for j in range(1, 8):
            hop2a(k, j).wait_recv()
        for n in range(4):
            hop2b(n, k * 2 + 1).wait_recv()

        @pl.when(i > 0)
        def _():
            for n in range(4):
                hop2b(n, k * 2).wait_recv()

        rows_a = ra[k]
        rows_b = rb[k]
        gate = across(rows_a, wg[:, :1024]) + across(rows_b, wg[:, 1024:])
        up = across(rows_a, wu[:, :1024]) + across(rows_b, wu[:, 1024:])
        hidden = (gate / (1.0 + jnp.exp(-gate)) * up).astype(BF)
        oa[k] = jnp.dot(hidden, wd[:, :1024], preferred_element_type=F32).astype(BF)
        ob[k] = jnp.dot(hidden, wd[:, 1024:], preferred_element_type=F32).astype(BF)
        for j in range(1, 8):
            hop3a(k, j).start()
        own3(k)[0].start()

        @pl.when(i > 0)
        def _():
            for j in (0, 2, 4, 6):
                hop3b(k, j).start()

        for j in (1, 3, 5, 7):
            hop3b(k, j).start()
        return carry

    def work_first():
        for j in range(4):
            own3(j)[1].start()

    lax.fori_loop(0, 1, work, 0)
    work_first()
    lax.fori_loop(1, 4, work, 0)

    def back(k, side):
        if side == 0:
            return rcopy(pa.at[k], qa.at[k], s4.at[0, k], r4.at[0, k], where_x(4 - k))
        return rcopy(pb.at[k], qb.at[k], s4.at[1, k], r4.at[1, k], where_y(4 - k))

    def weigh(slots, gates, k, rows):
        w = table(slots, k) * gates[k][:, None, :]
        w = w.reshape(256, 256)
        hi = w.astype(BF)
        lo = (w - hi.astype(F32)).astype(BF)
        dims = (((0,), (0,)), ((), ()))
        return lax.dot_general(hi, rows, dims, preferred_element_type=F32) + lax.dot_general(
            lo, rows, dims, preferred_element_type=F32
        )

    def home_a(i, carry):
        k = turn(i)
        for j in range(1, 8):
            hop3a(k, j).wait_recv()
        own3(k)[0].wait()
        pa[k] = weigh(sla, gta, k, ma[k]).astype(BF)
        back(k, 0).start()
        return carry

    def home_b(i, carry):
        k = turn(i)
        for n in range(4):
            hop3b(n, k * 2 + 1).wait_recv()
            if n:
                hop3b(n, k * 2).wait_recv()
        own3(k)[1].wait()
        pb[k] = weigh(slb, gtb, k, mb[k]).astype(BF)
        back(k, 1).start()
        return carry

    lax.fori_loop(1, 4, home_a, 0)
    lax.fori_loop(1, 4, home_b, 0)
    for j in range(1, 8):
        hop3a(0, j).wait_recv()
    own3(0)[0].wait()
    for n in range(4):
        hop3b(n, 1).wait_recv()
        if n:
            hop3b(n, 0).wait_recv()
    own3(0)[1].wait()
    total_a = weigh(sla, gta, 0, ma[0])
    total_b = weigh(slb, gtb, 0, mb[0])
    for k in (1, 3, 2):
        back(k, 0).wait_recv()
        back(k, 1).wait_recv()
        total_a += qa[k].astype(F32)
        total_b += qb[k].astype(F32)
    out[:, :1024] = total_a.astype(BF)
    out[:, 1024:] = total_b.astype(BF)

    for k in (1, 3):
        for cp in first(k) + onward(k):
            cp.wait_send()
    for k in (1, 2, 3):
        back(k, 0).wait_send()
        back(k, 1).wait_send()

    def drain(k, carry):
        for j in range(1, 8):
            hop2a(k, j).wait_send()
            hop2b(k, j).wait_send()
            hop3a(k, j).wait_send()
        for j in (1, 3, 5, 7):
            hop3b(k, j).wait_send()

        @pl.when(k > 0)
        def _():
            for j in (0, 2, 4, 6):
                hop3b(k, j).wait_send()

        return carry

    lax.fori_loop(0, 4, drain, 0)


def experts(column, slots, gates, wg, wu, wd):
    vm = pl.BlockSpec(memory_space=pltpu.VMEM)
    big = (4, 256, 1024)
    dma = pltpu.SemaphoreType.DMA
    return pl.pallas_call(
        experts_kernel,
        out_shape=jax.ShapeDtypeStruct((256, 2048), BF),
        in_specs=[vm] * 8,
        out_specs=vm,
        scratch_shapes=[pltpu.VMEM(big, BF)] * 14
        + [
            dma((2, 4)), dma((2, 4)),
            dma((4, 8)), dma((4, 8)), dma((4, 8)), dma((4, 8)),
            dma((4, 8)), dma((4, 8)), dma((4, 8)), dma((4, 8)),
            dma((2, 4)), dma((2, 4)),
            dma((16,)),
        ],
        compiler_params=pltpu.CompilerParams(
            collective_id=4, has_side_effects=True, vmem_limit_bytes=60 * 2**20
        ),
        name="experts",
    )(column, slots[0], slots[1], gates[0], gates[1], wg, wu, wd)


def slot_tables(rgs, z, y, x, c):
    routes = rgs[:, :, :, :6].transpose(0, 1, 3, 2, 4).reshape(2, 4, 6, 256).astype(jnp.int32)
    gates = rgs[:, :, :, 8:14].transpose(0, 1, 3, 2, 4).reshape(2, 4, 6, 256)
    off = jnp.arange(8, dtype=jnp.int32) // 2
    core = (c + jnp.arange(8, dtype=jnp.int32) % 2) % 2
    base = (z // 4) * 32
    expert = jnp.stack(
        [base + ((y + off) % 4) * 8 + x * 2 + core, base + y * 8 + ((x + off) % 4) * 2 + core]
    )
    hit = routes[:, :, None] == expert[:, None, :, None, None]
    member = jnp.any(hit, axis=3)
    gate = jnp.sum(jnp.where(hit, gates[:, :, None], 0.0), axis=3)
    ti = lax.broadcasted_iota(jnp.int32, (256, 256), 0)
    tj = lax.broadcasted_iota(jnp.int32, (256, 256), 1)
    before = ((ti < tj) & (tj // 32 == ti // 32)).astype(BF)
    rank = jnp.dot(
        member.astype(BF).reshape(64, 256), before, preferred_element_type=F32
    ).reshape(member.shape)
    token = lax.broadcasted_iota(jnp.int32, member.shape, 3)
    slot = jnp.where(member, (token // 32 * 4).astype(F32) + rank, -1.0)
    return slot, gate


def body(
    tokens, block_ids, attn_gain, q_weight, kv_weight, kv_gain, uk_weight, uv_weight,
    o_weight, ffn_gain, w_gate, w_up, w_down, routes, gate_weights,
):
    z, y, x, c = place()
    t = lax.axis_index("tp")
    s = lax.axis_index("seq")
    own_blocks = lax.dynamic_slice(block_ids, (s, 0), (1, 2))[0]
    normed_own = normalize(tokens, attn_gain).astype(BF)
    own_pos = own_blocks[t // 2] * 64 + (t % 2) * 32 + jnp.arange(32, dtype=jnp.int32)
    projected = jnp.dot(normed_own, kv_weight, preferred_element_type=F32)
    latent = normalize(projected[:, :512], kv_gain).astype(BF)
    key_rope = rotate(projected[:, 512:], own_pos).astype(BF)
    kv_own = jnp.concatenate([latent, key_rope, jnp.zeros((32, 64), BF)], axis=1)
    pad2 = jnp.zeros((2, 128), F32)
    rg = jnp.concatenate([routes.astype(F32).T, pad2, gate_weights.T, pad2], axis=0)
    kv, normed, rgs = gather_keys(kv_own, normed_own, rg)

    normed = normed.reshape(128, 2048)
    query_pos = (own_blocks[:, None] * 64 + jnp.arange(64, dtype=jnp.int32)[None, :]).reshape(128)
    queries = jnp.dot(normed, q_weight, preferred_element_type=F32).astype(BF)
    queries = queries.reshape(128, 4, 192)
    query_rope = rotate(queries[..., 128:].astype(F32), query_pos).astype(BF)
    query_latent = jnp.einsum(
        "thn,hln->hlt", queries[..., :128], uk_weight, preferred_element_type=F32
    ).astype(BF)
    q = jnp.concatenate(
        [query_latent, query_rope.transpose(1, 2, 0), jnp.zeros((4, 64, 128), BF)], axis=1
    )
    q = q.reshape(4, KEYW, 2, 64).transpose(2, 1, 0, 3).reshape(2, KEYW, 256)
    ids = jnp.arange(64, dtype=jnp.int32)
    inv = jnp.sum(
        jnp.where(block_ids[:, 0][None, :] == ids[:, None], ids[None, :], 0), axis=1
    ).astype(jnp.int32)
    out_latent = attention(inv, own_blocks[:1], q, kv.reshape(64, 128, KEYW))
    out_latent = out_latent.reshape(2, 4, 64, 512).transpose(1, 0, 2, 3).reshape(4, 128, 512)
    head_out = jnp.einsum(
        "htl,hlv->thv", out_latent, uv_weight, preferred_element_type=F32
    ).astype(BF)
    partial_out = jnp.dot(head_out.reshape(128, 512), o_weight, preferred_element_type=F32)
    parts = exchange(
        tp_scatter_kernel, "tp_scatter", 1, partial_out.astype(BF).reshape(4, 32, 2048),
        (4, 32, 2048),
    )
    attn_own = jnp.sum(parts.astype(F32), axis=0)
    mixed = (tokens.astype(F32) + attn_own).astype(BF)
    normed_ffn = normalize(mixed, ffn_gain).astype(BF)
    column = column_gather(normed_ffn).reshape(256, 2048)
    slots, gates = slot_tables(rgs, z, y, x, c)
    combined = experts(column, slots, gates, w_gate[0].T, w_up[0].T, w_down[0])
    sums = column_scatter(combined.reshape(8, 32, 2048))
    return (mixed.astype(F32) + sums).astype(BF)


def solution(mesh):
    return jax.shard_map(
        body,
        mesh=mesh,
        in_specs=(
            P(("seq", "tp"), None), P(), P(), P(None, "tp"), P(), P(),
            P("tp", None, None), P("tp", None, None), P("tp", None), P(),
            P("seq", None, "tp"), P("seq", None, "tp"), P("seq", "tp", None),
            P("seq", None), P("seq", None),
        ),
        out_specs=P(("seq", "tp"), None),
        check_vma=False,
    )
```

```python
import functools
import math

import jax
import jax.numpy as jnp
from jax import lax
from jax.experimental import pallas as pl
from jax.experimental.pallas import tpu as pltpu
from jax.sharding import PartitionSpec as P

EPSILON = 1e-06
MESH = pl.DeviceIdType.MESH
BF = jnp.bfloat16
F32 = jnp.float32
KEYW = 640


def place():
    s = lax.axis_index("seq")
    t = lax.axis_index("tp")
    return (s // 32) * 4 + t, (s // 8) % 4, (s // 2) % 4, s % 2


def dev(z, y, x, c):
    z, y, x, c = z % 8, y % 4, x % 4, c % 2
    return ((z // 4) * 32 + y * 8 + x * 2 + c, z % 4)


def greet(peers):
    barrier = pltpu.get_barrier_semaphore()
    for p in peers:
        pl.semaphore_signal(barrier, inc=1, device_id=p, device_id_type=MESH)
    pl.semaphore_wait(barrier, len(peers))


def rcopy(src, dst, ss, rs, device):
    return pltpu.make_async_remote_copy(
        src_ref=src, dst_ref=dst, send_sem=ss, recv_sem=rs, device_id=device, device_id_type=MESH
    )


def normalize(values, gain_vec):
    values = values.astype(F32)
    factor = lax.rsqrt(jnp.mean(values * values, axis=-1, keepdims=True) + EPSILON)
    return values * factor * gain_vec


def rotate(values, position):
    half_width = values.shape[-1] // 2
    frequency = jnp.exp(
        jnp.arange(half_width, dtype=F32) * (-2.0 * math.log(10000.0) / values.shape[-1])
    )
    angles = position.astype(F32).reshape(position.shape + (1,) * (values.ndim - 1)) * frequency
    cosine = jnp.cos(angles)
    sine_part = jnp.sin(angles)
    first_half = values[..., :half_width]
    second_half = values[..., half_width:]
    return jnp.concatenate(
        [
            first_half * cosine - second_half * sine_part,
            second_half * cosine + first_half * sine_part,
        ],
        axis=-1,
    )


def gather_kernel(kv_ref, nt_ref, rg_ref, KV, NT, RG, ssem, rsem, lsem):
    z, y, x, c = place()
    zh, t = z // 4, z % 4
    peers = [dev(z + k, y, x, c) for k in range(1, 8)]
    xs = [dev(z, y, x + 1, c), dev(z, y, x + 3, c), dev(z, y, x + 2, c)]
    ys = [dev(z, y + 1, x, c), dev(z, y + 3, x, c), dev(z, y + 2, x, c)]
    other = dev(z, y, x, c + 1)
    greet(peers + xs + ys + [other])
    number = [0]
    sent = []

    def send(src, dst, device):
        i = number[0]
        number[0] += 1
        cp = rcopy(src, dst, ssem.at[i], rsem.at[i], device)
        cp.start()
        sent.append(cp)
        return i

    def arrived(i, region):
        rcopy(region, region, ssem.at[i], rsem.at[i], other).wait_recv()

    rows = pl.ds(pl.multiple_of(t * 32, 32), 32)
    zi = {}
    mine = KV.at[zh, y, x, c, rows]
    for k in (4, 3, 5, 2, 6, 1, 7):
        zi[k] = send(kv_ref, mine, dev(z + k, y, x, c))
    locals_ = [
        pltpu.make_async_copy(kv_ref, mine, lsem.at[0]),
        pltpu.make_async_copy(nt_ref, NT.at[t], lsem.at[1]),
        pltpu.make_async_copy(rg_ref, RG.at[0, 0, zh], lsem.at[2]),
    ]
    for cp in locals_:
        cp.start()
    ri = send(rg_ref, RG.at[0, 0, zh], dev(z + 4, y, x, c))
    ti = {}
    for k in (3, 2, 1):
        ti[k] = send(nt_ref, NT.at[t], (zh * 32 + y * 8 + x * 2 + c, (t + k) % 4))
    for cp in locals_:
        cp.wait()
    for k in zi:
        zz = (z - k + 8) % 8
        arrived(zi[k], KV.at[zz // 4, y, x, c, pl.ds(pl.multiple_of((zz % 4) * 32, 32), 32)])
    arrived(ri, RG.at[0, 0, 1 - zh])
    spare = pltpu.make_async_copy(RG.at[0, 0], RG.at[1, 0], lsem.at[2])
    spare.start()
    routes_sent = []
    for k in (1, 2, 3):
        g = RG.at[0, 0]
        routes_sent.append((send(g, RG.at[0, k], dev(z, y, x + k, c)), RG.at[0, k]))
        routes_sent.append((send(g, RG.at[1, k], dev(z, y + k, x, c)), RG.at[1, k]))
    lo, hi = pl.ds(0, 64), pl.ds(64, 64)
    xm, xp, xo = (x + 3) % 4, (x + 1) % 4, (x + 2) % 4
    ym, yp, yo = (y + 3) % 4, (y + 1) % 4, (y + 2) % 4
    a, b = KV.at[0, y, x, c], KV.at[1, y, x, c]
    ap = send(a, a, xs[0])
    am = send(a, a, xs[1])
    bp = send(b, b, ys[0])
    bm = send(b, b, ys[1])
    arrived(ap, KV.at[0, y, xm, c])
    g = KV.at[0, y, xm, c, lo]
    ap2 = send(g, g, xs[0])
    arrived(bp, KV.at[1, ym, x, c])
    g = KV.at[1, ym, x, c, lo]
    bp2 = send(g, g, ys[0])
    arrived(am, KV.at[0, y, xp, c])
    g = KV.at[0, y, xp, c, hi]
    am2 = send(g, g, xs[1])
    arrived(bm, KV.at[1, yp, x, c])
    g = KV.at[1, yp, x, c, hi]
    bm2 = send(g, g, ys[1])
    arrived(ap2, KV.at[0, y, xo, c, lo])
    arrived(am2, KV.at[0, y, xo, c, hi])
    r = KV.at[0, y, :, c]
    rp = send(r, r, ys[0])
    rm = send(r, r, ys[1])
    arrived(bp2, KV.at[1, yo, x, c, lo])
    arrived(bm2, KV.at[1, yo, x, c, hi])
    q = KV.at[1, :, x, c]
    qp = send(q, q, xs[0])
    qm = send(q, q, xs[1])
    across = [send(r, r, other), send(q, q, other)]
    arrived(rp, KV.at[0, ym, :, c])
    g = KV.at[0, ym, :, c, lo]
    rp2 = send(g, g, ys[0])
    arrived(qp, KV.at[1, :, xm, c])
    g = KV.at[1, :, xm, c, lo]
    qp2 = send(g, g, xs[0])
    arrived(rm, KV.at[0, yp, :, c])
    g = KV.at[0, yp, :, c, hi]
    rm2 = send(g, g, ys[1])
    arrived(qm, KV.at[1, :, xp, c])
    g = KV.at[1, :, xp, c, hi]
    qm2 = send(g, g, xs[1])
    for g in (KV.at[0, ym, :, c], KV.at[1, :, xm, c], KV.at[0, yp, :, c], KV.at[1, :, xp, c]):
        across.append(send(g, g, other))
    arrived(rp2, KV.at[0, yo, :, c, lo])
    arrived(rm2, KV.at[0, yo, :, c, hi])
    g = KV.at[0, yo, :, c]
    across.append(send(g, g, other))
    arrived(qp2, KV.at[1, :, xo, c, lo])
    arrived(qm2, KV.at[1, :, xo, c, hi])
    g = KV.at[1, :, xo, c]
    across.append(send(g, g, other))
    d = 1 - c
    for i, region in zip(
        across,
        (
            KV.at[0, y, :, d],
            KV.at[1, :, x, d],
            KV.at[0, ym, :, d],
            KV.at[1, :, xm, d],
            KV.at[0, yp, :, d],
            KV.at[1, :, xp, d],
            KV.at[0, yo, :, d],
            KV.at[1, :, xo, d],
        ),
    ):
        arrived(i, region)
    for k in ti:
        arrived(ti[k], NT.at[(t - k + 4) % 4])
    spare.wait()
    for i, region in routes_sent:
        arrived(i, region)
    for cp in sent:
        cp.wait_send()


def gather_keys(kv_own, normed_own, rg):
    count = 48
    vm = pl.BlockSpec(memory_space=pltpu.VMEM)
    return pl.pallas_call(
        gather_kernel,
        out_shape=(
            jax.ShapeDtypeStruct((2, 4, 4, 2, 128, KEYW), BF),
            jax.ShapeDtypeStruct((4, 32, 2048), BF),
            jax.ShapeDtypeStruct((2, 4, 2, 16, 128), F32),
        ),
        in_specs=[vm, vm, vm],
        out_specs=(pl.BlockSpec(memory_space=pltpu.HBM), vm, vm),
        scratch_shapes=[
            pltpu.SemaphoreType.DMA((count,)),
            pltpu.SemaphoreType.DMA((count,)),
            pltpu.SemaphoreType.DMA((3,)),
        ],
        compiler_params=pltpu.CompilerParams(
            collective_id=0, has_side_effects=True, vmem_limit_bytes=60 * 2**20
        ),
        name="gather_keys",
    )(kv_own, normed_own, rg)


CHUNK = 1024


def attention_kernel(inv_ref, blk_ref, q_ref, kv_hbm, o_ref, kbuf, m_ref, l_ref, acc_ref, sems):
    low = blk_ref[0]
    per = CHUNK // 64
    top_chunks = (127 - low) // per + 1

    def issue(p, carry):
        second = p >= 64
        d = inv_ref[jnp.where(second, 127 - p, p)]
        off = pl.multiple_of(jnp.where(second, 64, 0), 64)
        pltpu.make_async_copy(
            kv_hbm.at[d, pl.ds(off, 64)],
            kbuf.at[pl.ds(pl.multiple_of(p * 64, 64), 64)],
            sems.at[p // per],
        ).start()
        return carry

    lax.fori_loop(0, top_chunks * per, issue, 0)
    scale = (128 + 64) ** (-0.5)

    for half in (1, 0):
        block = low if half == 0 else 127 - low
        last = block // per
        m_ref[...] = jnp.full_like(m_ref, -1e30)
        l_ref[...] = jnp.zeros_like(l_ref)
        acc_ref[...] = jnp.zeros_like(acc_ref)

        def step(ch, masked):
            region = kbuf.at[pl.ds(pl.multiple_of(ch * CHUNK, CHUNK), CHUNK)]
            if half == 1:
                pltpu.make_async_copy(region, region, sems.at[ch]).wait()
            keys = region[...]
            s = jnp.dot(keys, q_ref[half], preferred_element_type=F32) * scale
            if masked:
                key = lax.broadcasted_iota(jnp.int32, s.shape, 0)
                query = lax.broadcasted_iota(jnp.int32, s.shape, 1) % 64
                s = jnp.where(key - query <= block * 64 - ch * CHUNK, s, -1e30)
            m_old = m_ref[...]
            m_new = jnp.maximum(m_old, jnp.max(s, axis=0, keepdims=True))
            p = jnp.exp(s - m_new)
            alpha = jnp.exp(m_old - m_new)
            l_ref[...] = l_ref[...] * alpha + jnp.sum(p, axis=0, keepdims=True)
            m_ref[...] = m_new
            acc_ref[...] = acc_ref[...] * alpha + lax.dot_general(
                keys[:, :512], p.astype(BF), (((0,), (0,)), ((), ())), preferred_element_type=F32
            )

        def loop(ch, carry):
            step(ch, False)
            return carry

        lax.fori_loop(0, last, loop, 0)
        step(last, True)
        o_ref[half] = (acc_ref[...] / l_ref[...]).T.astype(BF)


def attention(inv, low, q, kv):
    return pl.pallas_call(
        attention_kernel,
        out_shape=jax.ShapeDtypeStruct((2, 256, 512), BF),
        in_specs=[
            pl.BlockSpec(memory_space=pltpu.SMEM),
            pl.BlockSpec(memory_space=pltpu.SMEM),
            pl.BlockSpec(memory_space=pltpu.VMEM),
            pl.BlockSpec(memory_space=pltpu.HBM),
        ],
        out_specs=pl.BlockSpec(memory_space=pltpu.VMEM),
        scratch_shapes=[
            pltpu.VMEM((8192, KEYW), BF),
            pltpu.VMEM((1, 256), F32),
            pltpu.VMEM((1, 256), F32),
            pltpu.VMEM((512, 256), F32),
            pltpu.SemaphoreType.DMA((8192 // CHUNK,)),
        ],
        compiler_params=pltpu.CompilerParams(vmem_limit_bytes=60 * 2**20),
        name="attention",
    )(inv, low, q, kv)


def tp_scatter_kernel(p_ref, o_ref, ssem, rsem, lsem):
    z, y, x, c = place()
    s, t = lax.axis_index("seq"), lax.axis_index("tp")
    greet([(s, (t + k) % 4) for k in (1, 2, 3)])
    cps = []
    for k in (2, 3, 1):
        to = (t + k) % 4
        cp = rcopy(p_ref.at[to], o_ref.at[k], ssem.at[k], rsem.at[k], (s, to))
        cp.start()
        cps.append(cp)
    own = pltpu.make_async_copy(p_ref.at[t], o_ref.at[0], lsem)
    own.start()
    own.wait()
    for cp in cps:
        cp.wait()


def column_gather_kernel(p_ref, o_ref, ssem, rsem, lsem):
    z, y, x, c = place()
    towards = (dev(z + 1, y, x, c), dev(z + 7, y, x, c))
    greet(towards)

    def shard(d, s):
        return (z + 8 - s) % 8 if d == 0 else (z + s) % 8

    def hop(d, s, h):
        rows = pl.ds(h * 16, 16)
        src = p_ref.at[rows] if s == 1 else o_ref.at[shard(d, s - 1), rows]
        return rcopy(
            src, o_ref.at[shard(d, s - 1), rows], ssem.at[d, s - 1, h], rsem.at[d, s - 1, h],
            towards[d],
        )

    def arrived(d, s, h):
        region = o_ref.at[shard(d, s), pl.ds(h * 16, 16)]
        rcopy(region, region, ssem.at[d, s - 1, h], rsem.at[d, s - 1, h], towards[d]).wait_recv()

    for h in (0, 1):
        for d in (0, 1):
            hop(d, 1, h).start()
    own = pltpu.make_async_copy(p_ref, o_ref.at[z], lsem)
    own.start()
    for s in (2, 3, 4):
        for h in (0, 1):
            for d in (0, 1):
                arrived(d, s - 1, h)
                if s < 4 or h == d:
                    hop(d, s, h).start()
    own.wait()
    for d in (0, 1):
        arrived(d, 4, d)
        for s in (1, 2, 3):
            for h in (0, 1):
                hop(d, s, h).wait_send()
        hop(d, 4, d).wait_send()


def column_gather(array):
    vm = pl.BlockSpec(memory_space=pltpu.VMEM)
    return pl.pallas_call(
        column_gather_kernel,
        out_shape=jax.ShapeDtypeStruct((8, 32, 2048), BF),
        in_specs=[vm],
        out_specs=vm,
        scratch_shapes=[
            pltpu.SemaphoreType.DMA((2, 4, 2)),
            pltpu.SemaphoreType.DMA((2, 4, 2)),
            pltpu.SemaphoreType.DMA,
        ],
        compiler_params=pltpu.CompilerParams(
            collective_id=2, has_side_effects=True, vmem_limit_bytes=16 * 2**20
        ),
        name="column_gather",
    )(array)


def column_scatter_kernel(p_ref, o_ref, rbuf, sbuf, ssem, rsem):
    z, y, x, c = place()
    towards = (dev(z + 1, y, x, c), dev(z + 7, y, x, c))
    greet(towards)

    def target(d, s):
        return (z + 5 - s) % 8 if d == 0 else (z + 3 + s) % 8

    def hop(d, s, h, src):
        rows = pl.ds(h * 16, 16)
        return rcopy(
            src.at[rows], rbuf.at[d, s - 1, rows], ssem.at[d, s - 1, h], rsem.at[d, s - 1, h],
            towards[d],
        )

    started = []
    for d in (0, 1):
        cp = hop(d, 1, d, p_ref.at[target(d, 1)])
        cp.start()
        started.append(cp)
    for d in (0, 1):
        cp = hop(d, 2, 1 - d, p_ref.at[target(d, 2)])
        cp.start()
        started.append(cp)
    for s in (2, 3, 4):
        for h in (0, 1):
            todo = []
            for d in (0, 1):
                if s == 2 and h != d:
                    continue
                rows = pl.ds(h * 16, 16)
                hop(d, s - 1, h, sbuf.at[d, s - 1]).wait_recv()
                sbuf[d, s - 1, rows] = (
                    p_ref[target(d, s), rows].astype(F32) + rbuf[d, s - 2, rows].astype(F32)
                ).astype(BF)
                todo.append(hop(d, s, h, sbuf.at[d, s - 1]))
            for cp in todo:
                cp.start()
                started.append(cp)
    for h in (0, 1):
        for d in (0, 1):
            hop(d, 4, h, sbuf.at[d, 3]).wait_recv()
    o_ref[...] = (
        p_ref[z].astype(F32) + rbuf[0, 3].astype(F32) + rbuf[1, 3].astype(F32)
    )
    for cp in started:
        cp.wait_send()


def column_scatter(array):
    vm = pl.BlockSpec(memory_space=pltpu.VMEM)
    return pl.pallas_call(
        column_scatter_kernel,
        out_shape=jax.ShapeDtypeStruct((32, 2048), F32),
        in_specs=[vm],
        out_specs=vm,
        scratch_shapes=[
            pltpu.VMEM((2, 4, 32, 2048), BF),
            pltpu.VMEM((2, 4, 32, 2048), BF),
            pltpu.SemaphoreType.DMA((2, 4, 2)),
            pltpu.SemaphoreType.DMA((2, 4, 2)),
        ],
        compiler_params=pltpu.CompilerParams(
            collective_id=3, has_side_effects=True, vmem_limit_bytes=16 * 2**20
        ),
        name="column_scatter",
    )(array)


def exchange(kernel, name, cid, array, out):
    vm = pl.BlockSpec(memory_space=pltpu.VMEM)
    return pl.pallas_call(
        kernel,
        out_shape=jax.ShapeDtypeStruct(out, BF),
        in_specs=[vm],
        out_specs=vm,
        scratch_shapes=[
            pltpu.SemaphoreType.DMA((8,)),
            pltpu.SemaphoreType.DMA((8,)),
            pltpu.SemaphoreType.DMA,
        ],
        compiler_params=pltpu.CompilerParams(
            collective_id=cid, has_side_effects=True, vmem_limit_bytes=16 * 2**20
        ),
        name=name,
    )(array)


def turn(i):
    return ((i * (i + 1)) // 2) % 4


def experts_kernel(
    xin, sla, slb, gta, gtb, wg, wu, wd, out,
    ta, tb, sa, sb, ra, rb, oa, ob, ma, mb, pa, pb, qa, qb,
    s1, r1, s2a, r2a, s2b, r2b, s3a, r3a, s3b, r3b, s4, r4, lsem,
):
    z, y, x, c = place()
    peers = [dev(z, y, x, c + 1)]
    for k in (1, 2, 3):
        for d in (0, 1):
            peers.append(dev(z, y + k, x, c + d))
            peers.append(dev(z, y, x + k, c + d))
    greet(peers)
    left, right = pl.ds(0, 1024), pl.ds(1024, 1024)
    low, high = pl.ds(0, 128), pl.ds(128, 128)

    def blk(j):
        return pl.ds(pl.multiple_of(j * 32, 32), 32)

    def where_x(k):
        return dev(z, y, x + k, c)

    def where_y(k):
        return dev(z, y + k, x, c)

    def first(k):
        return (
            rcopy(xin.at[:, left], ta.at[k], s1.at[0, k], r1.at[0, k], where_x(k)),
            rcopy(xin.at[:, right], tb.at[k], s1.at[1, k], r1.at[1, k], where_y(k)),
        )

    def onward(k):
        rows, i = (low, 2) if k == 1 else (high, 0)
        return (
            rcopy(ta.at[k, rows], ta.at[2, rows], s1.at[0, i], r1.at[0, i], where_x(k)),
            rcopy(tb.at[k, rows], tb.at[2, rows], s1.at[1, i], r1.at[1, i], where_y(k)),
        )

    for k in (1, 3):
        for cp in first(k):
            cp.start()
    ta[0] = xin[:, :1024]
    tb[0] = xin[:, 1024:]

    def hop2a(k, j):
        return rcopy(
            sa.at[k, blk(j)], ra.at[k, blk(j)], s2a.at[k, j], r2a.at[k, j],
            dev(z, y + j // 2, x, c + j % 2),
        )

    def hop2b(k, j):
        return rcopy(
            sb.at[k, blk(j)], rb.at[j // 2, blk(k * 2 + j % 2)], s2b.at[k, j], r2b.at[k, j],
            dev(z, y, x + j // 2, c + j % 2),
        )

    def own2(k):
        return (
            pltpu.make_async_copy(sa.at[k, blk(0)], ra.at[k, blk(0)], lsem.at[k]),
            pltpu.make_async_copy(sb.at[k, blk(0)], rb.at[0, blk(k * 2)], lsem.at[4 + k]),
        )

    number = lax.broadcasted_iota(jnp.int32, (8, 32, 256), 1).astype(F32)

    def table(slots, k):
        return (slots[k][:, None, :] == number).astype(F32)

    def spread(i, carry):
        k = turn(i)

        @pl.when(i == 1)
        def _():
            for n in (1, 3):
                for cp, cp2 in zip(first(n), onward(n)):
                    cp.wait_recv()
                    cp2.start()

        @pl.when(i == 3)
        def _():
            for n in (1, 3):
                for cp in onward(n):
                    cp.wait_recv()

        sa[k] = jnp.dot(
            table(sla, k).reshape(256, 256).astype(BF), ta[k], preferred_element_type=F32
        ).astype(BF)
        sb[k] = jnp.dot(
            table(slb, k).reshape(256, 256).astype(BF), tb[k], preferred_element_type=F32
        ).astype(BF)
        for j in (2, 6, 4, 3, 7, 5, 1):
            hop2a(k, j).start()
            hop2b(k, j).start()
        for cp in own2(k):
            cp.start()
        return carry

    lax.fori_loop(0, 4, spread, 0)

    def hop3a(k, j):
        return rcopy(
            oa.at[k, blk(j)], ma.at[k, blk(j)], s3a.at[k, j], r3a.at[k, j],
            dev(z, y + 4 - j // 2, x, c + j % 2),
        )

    def hop3b(k, j):
        return rcopy(
            ob.at[k, blk(j)], mb.at[j // 2, blk(k * 2 + j % 2)], s3b.at[k, j], r3b.at[k, j],
            dev(z, y, x + 4 - k, c + j % 2),
        )

    def own3(k):
        return (
            pltpu.make_async_copy(oa.at[k, blk(0)], ma.at[k, blk(0)], lsem.at[8 + k]),
            pltpu.make_async_copy(ob.at[0, blk(k * 2)], mb.at[k, blk(0)], lsem.at[12 + k]),
        )

    for k in range(4):
        for cp in own2(k):
            cp.wait()

    def across(rows, weight):
        return lax.dot_general(
            rows, weight, (((1,), (1,)), ((), ())), preferred_element_type=F32
        )

    def work(i, carry):
        k = turn(i)
        for j in range(1, 8):
            hop2a(k, j).wait_recv()
        for n in range(4):
            hop2b(n, k * 2 + 1).wait_recv()

        @pl.when(i > 0)
        def _():
            for n in range(4):
                hop2b(n, k * 2).wait_recv()

        rows_a = ra[k]
        rows_b = rb[k]
        gate = across(rows_a, wg[:, :1024]) + across(rows_b, wg[:, 1024:])
        up = across(rows_a, wu[:, :1024]) + across(rows_b, wu[:, 1024:])
        hidden = (gate / (1.0 + jnp.exp(-gate)) * up).astype(BF)
        oa[k] = jnp.dot(hidden, wd[:, :1024], preferred_element_type=F32).astype(BF)
        ob[k] = jnp.dot(hidden, wd[:, 1024:], preferred_element_type=F32).astype(BF)
        for j in range(1, 8):
            hop3a(k, j).start()
        own3(k)[0].start()

        @pl.when(i > 0)
        def _():
            for j in (0, 2, 4, 6):
                hop3b(k, j).start()

        for j in (1, 3, 5, 7):
            hop3b(k, j).start()
        return carry

    def work_first():
        for j in range(4):
            own3(j)[1].start()

    lax.fori_loop(0, 1, work, 0)
    work_first()
    lax.fori_loop(1, 4, work, 0)

    def back(k, side):
        if side == 0:
            return rcopy(pa.at[k], qa.at[k], s4.at[0, k], r4.at[0, k], where_x(4 - k))
        return rcopy(pb.at[k], qb.at[k], s4.at[1, k], r4.at[1, k], where_y(4 - k))

    def weigh(slots, gates, k, rows):
        w = table(slots, k) * gates[k][:, None, :]
        w = w.reshape(256, 256)
        hi = w.astype(BF)
        lo = (w - hi.astype(F32)).astype(BF)
        dims = (((0,), (0,)), ((), ()))
        return lax.dot_general(hi, rows, dims, preferred_element_type=F32) + lax.dot_general(
            lo, rows, dims, preferred_element_type=F32
        )

    def home_a(i, carry):
        k = turn(i)
        for j in range(1, 8):
            hop3a(k, j).wait_recv()
        own3(k)[0].wait()
        pa[k] = weigh(sla, gta, k, ma[k]).astype(BF)
        back(k, 0).start()
        return carry

    def home_b(i, carry):
        k = turn(i)
        for n in range(4):
            hop3b(n, k * 2 + 1).wait_recv()
            if n:
                hop3b(n, k * 2).wait_recv()
        own3(k)[1].wait()
        pb[k] = weigh(slb, gtb, k, mb[k]).astype(BF)
        back(k, 1).start()
        return carry

    lax.fori_loop(1, 4, home_a, 0)
    lax.fori_loop(1, 4, home_b, 0)
    for j in range(1, 8):
        hop3a(0, j).wait_recv()
    own3(0)[0].wait()
    for n in range(4):
        hop3b(n, 1).wait_recv()
        if n:
            hop3b(n, 0).wait_recv()
    own3(0)[1].wait()
    total_a = weigh(sla, gta, 0, ma[0])
    total_b = weigh(slb, gtb, 0, mb[0])
    for k in (1, 3, 2):
        back(k, 0).wait_recv()
        back(k, 1).wait_recv()
        total_a += qa[k].astype(F32)
        total_b += qb[k].astype(F32)
    out[:, :1024] = total_a.astype(BF)
    out[:, 1024:] = total_b.astype(BF)

    for k in (1, 3):
        for cp in first(k) + onward(k):
            cp.wait_send()
    for k in (1, 2, 3):
        back(k, 0).wait_send()
        back(k, 1).wait_send()

    def drain(k, carry):
        for j in range(1, 8):
            hop2a(k, j).wait_send()
            hop2b(k, j).wait_send()
            hop3a(k, j).wait_send()
        for j in (1, 3, 5, 7):
            hop3b(k, j).wait_send()

        @pl.when(k > 0)
        def _():
            for j in (0, 2, 4, 6):
                hop3b(k, j).wait_send()

        return carry

    lax.fori_loop(0, 4, drain, 0)


def experts(column, slots, gates, wg, wu, wd):
    vm = pl.BlockSpec(memory_space=pltpu.VMEM)
    big = (4, 256, 1024)
    dma = pltpu.SemaphoreType.DMA
    return pl.pallas_call(
        experts_kernel,
        out_shape=jax.ShapeDtypeStruct((256, 2048), BF),
        in_specs=[vm] * 8,
        out_specs=vm,
        scratch_shapes=[pltpu.VMEM(big, BF)] * 14
        + [
            dma((2, 4)), dma((2, 4)),
            dma((4, 8)), dma((4, 8)), dma((4, 8)), dma((4, 8)),
            dma((4, 8)), dma((4, 8)), dma((4, 8)), dma((4, 8)),
            dma((2, 4)), dma((2, 4)),
            dma((16,)),
        ],
        compiler_params=pltpu.CompilerParams(
            collective_id=4, has_side_effects=True, vmem_limit_bytes=60 * 2**20
        ),
        name="experts",
    )(column, slots[0], slots[1], gates[0], gates[1], wg, wu, wd)


def slot_tables(rgs, z, y, x, c):
    routes = rgs[:, :, :, :6].transpose(0, 1, 3, 2, 4).reshape(2, 4, 6, 256).astype(jnp.int32)
    gates = rgs[:, :, :, 8:14].transpose(0, 1, 3, 2, 4).reshape(2, 4, 6, 256)
    off = jnp.arange(8, dtype=jnp.int32) // 2
    core = (c + jnp.arange(8, dtype=jnp.int32) % 2) % 2
    base = (z // 4) * 32
    expert = jnp.stack(
        [base + ((y + off) % 4) * 8 + x * 2 + core, base + y * 8 + ((x + off) % 4) * 2 + core]
    )
    hit = routes[:, :, None] == expert[:, None, :, None, None]
    member = jnp.any(hit, axis=3)
    gate = jnp.sum(jnp.where(hit, gates[:, :, None], 0.0), axis=3)
    ti = lax.broadcasted_iota(jnp.int32, (256, 256), 0)
    tj = lax.broadcasted_iota(jnp.int32, (256, 256), 1)
    before = ((ti < tj) & (tj // 32 == ti // 32)).astype(BF)
    rank = jnp.dot(
        member.astype(BF).reshape(64, 256), before, preferred_element_type=F32
    ).reshape(member.shape)
    token = lax.broadcasted_iota(jnp.int32, member.shape, 3)
    slot = jnp.where(member, (token // 32 * 4).astype(F32) + rank, -1.0)
    return slot, gate


def body(
    tokens, block_ids, attn_gain, q_weight, kv_weight, kv_gain, uk_weight, uv_weight,
    o_weight, ffn_gain, w_gate, w_up, w_down, routes, gate_weights,
):
    z, y, x, c = place()
    t = lax.axis_index("tp")
    s = lax.axis_index("seq")
    own_blocks = lax.dynamic_slice(block_ids, (s, 0), (1, 2))[0]
    normed_own = normalize(tokens, attn_gain).astype(BF)
    own_pos = own_blocks[t // 2] * 64 + (t % 2) * 32 + jnp.arange(32, dtype=jnp.int32)
    projected = jnp.dot(normed_own, kv_weight, preferred_element_type=F32)
    latent = normalize(projected[:, :512], kv_gain).astype(BF)
    key_rope = rotate(projected[:, 512:], own_pos).astype(BF)
    kv_own = jnp.concatenate([latent, key_rope, jnp.zeros((32, 64), BF)], axis=1)
    pad2 = jnp.zeros((2, 128), F32)
    rg = jnp.concatenate([routes.astype(F32).T, pad2, gate_weights.T, pad2], axis=0)
    kv, normed, rgs = gather_keys(kv_own, normed_own, rg)

    normed = normed.reshape(128, 2048)
    query_pos = (own_blocks[:, None] * 64 + jnp.arange(64, dtype=jnp.int32)[None, :]).reshape(128)
    queries = jnp.dot(normed, q_weight, preferred_element_type=F32).astype(BF)
    queries = queries.reshape(128, 4, 192)
    query_rope = rotate(queries[..., 128:].astype(F32), query_pos).astype(BF)
    query_latent = jnp.einsum(
        "thn,hln->hlt", queries[..., :128], uk_weight, preferred_element_type=F32
    ).astype(BF)
    q = jnp.concatenate(
        [query_latent, query_rope.transpose(1, 2, 0), jnp.zeros((4, 64, 128), BF)], axis=1
    )
    q = q.reshape(4, KEYW, 2, 64).transpose(2, 1, 0, 3).reshape(2, KEYW, 256)
    ids = jnp.arange(64, dtype=jnp.int32)
    inv = jnp.sum(
        jnp.where(block_ids[:, 0][None, :] == ids[:, None], ids[None, :], 0), axis=1
    ).astype(jnp.int32)
    out_latent = attention(inv, own_blocks[:1], q, kv.reshape(64, 128, KEYW))
    out_latent = out_latent.reshape(2, 4, 64, 512).transpose(1, 0, 2, 3).reshape(4, 128, 512)
    head_out = jnp.einsum(
        "htl,hlv->thv", out_latent, uv_weight, preferred_element_type=F32
    ).astype(BF)
    partial_out = jnp.dot(head_out.reshape(128, 512), o_weight, preferred_element_type=F32)
    parts = exchange(
        tp_scatter_kernel, "tp_scatter", 1, partial_out.astype(BF).reshape(4, 32, 2048),
        (4, 32, 2048),
    )
    attn_own = jnp.sum(parts.astype(F32), axis=0)
    mixed = (tokens.astype(F32) + attn_own).astype(BF)
    normed_ffn = normalize(mixed, ffn_gain).astype(BF)
    column = column_gather(normed_ffn).reshape(256, 2048)
    slots, gates = slot_tables(rgs, z, y, x, c)
    combined = experts(column, slots, gates, w_gate[0].T, w_up[0].T, w_down[0])
    sums = column_scatter(combined.reshape(8, 32, 2048))
    return (mixed.astype(F32) + sums).astype(BF)


def solution(mesh):
    return jax.shard_map(
        body,
        mesh=mesh,
        in_specs=(
            P(("seq", "tp"), None), P(), P(), P(None, "tp"), P(), P(),
            P("tp", None, None), P("tp", None, None), P("tp", None), P(),
            P("seq", None, "tp"), P("seq", None, "tp"), P("seq", "tp", None),
            P("seq", None), P("seq", None),
        ),
        out_specs=P(("seq", "tp"), None),
        check_vma=False,
    )
```

```python
import functools
import math

import jax
import jax.numpy as jnp
from jax import lax
from jax.experimental import pallas as pl
from jax.experimental.pallas import tpu as pltpu
from jax.sharding import PartitionSpec as P

EPSILON = 1e-06
MESH = pl.DeviceIdType.MESH
BF = jnp.bfloat16
F32 = jnp.float32
KEYW = 640


def place():
    s = lax.axis_index("seq")
    t = lax.axis_index("tp")
    return (s // 32) * 4 + t, (s // 8) % 4, (s // 2) % 4, s % 2


def dev(z, y, x, c):
    z, y, x, c = z % 8, y % 4, x % 4, c % 2
    return ((z // 4) * 32 + y * 8 + x * 2 + c, z % 4)


def greet(peers):
    barrier = pltpu.get_barrier_semaphore()
    for p in peers:
        pl.semaphore_signal(barrier, inc=1, device_id=p, device_id_type=MESH)
    pl.semaphore_wait(barrier, len(peers))


def rcopy(src, dst, ss, rs, device):
    return pltpu.make_async_remote_copy(
        src_ref=src, dst_ref=dst, send_sem=ss, recv_sem=rs, device_id=device, device_id_type=MESH
    )


def normalize(values, gain_vec):
    values = values.astype(F32)
    factor = lax.rsqrt(jnp.mean(values * values, axis=-1, keepdims=True) + EPSILON)
    return values * factor * gain_vec


def rotate(values, position):
    half_width = values.shape[-1] // 2
    frequency = jnp.exp(
        jnp.arange(half_width, dtype=F32) * (-2.0 * math.log(10000.0) / values.shape[-1])
    )
    angles = position.astype(F32).reshape(position.shape + (1,) * (values.ndim - 1)) * frequency
    cosine = jnp.cos(angles)
    sine_part = jnp.sin(angles)
    first_half = values[..., :half_width]
    second_half = values[..., half_width:]
    return jnp.concatenate(
        [
            first_half * cosine - second_half * sine_part,
            second_half * cosine + first_half * sine_part,
        ],
        axis=-1,
    )


def gather_kernel(
    kv_ref, nt_ref, rg_ref, qw_ref, uk_ref, cos_ref, sin_ref, KV, QO, RG, NT, ssem, rsem, lsem
):
    z, y, x, c = place()
    zh, t = z // 4, z % 4
    peers = [dev(z + k, y, x, c) for k in range(1, 8)]
    xs = [dev(z, y, x + 1, c), dev(z, y, x + 3, c), dev(z, y, x + 2, c)]
    ys = [dev(z, y + 1, x, c), dev(z, y + 3, x, c), dev(z, y + 2, x, c)]
    other = dev(z, y, x, c + 1)
    greet(peers + xs + ys + [other])
    number = [0]
    sent = []

    def send(src, dst, device):
        i = number[0]
        number[0] += 1
        cp = rcopy(src, dst, ssem.at[i], rsem.at[i], device)
        cp.start()
        sent.append(cp)
        return i

    def arrived(i, region):
        rcopy(region, region, ssem.at[i], rsem.at[i], other).wait_recv()

    rows = pl.ds(pl.multiple_of(t * 32, 32), 32)
    zi = {}
    mine = KV.at[zh, y, x, c, rows]
    for k in (4, 3, 5, 2, 6, 1, 7):
        zi[k] = send(kv_ref, mine, dev(z + k, y, x, c))
    locals_ = [
        pltpu.make_async_copy(kv_ref, mine, lsem.at[0]),
        pltpu.make_async_copy(nt_ref, NT.at[t], lsem.at[1]),
        pltpu.make_async_copy(rg_ref, RG.at[0, 0, zh], lsem.at[2]),
    ]
    for cp in locals_:
        cp.start()
    ri = send(rg_ref, RG.at[0, 0, zh], dev(z + 4, y, x, c))
    ti = {}
    for k in (3, 2, 1):
        ti[k] = send(nt_ref, NT.at[t], (zh * 32 + y * 8 + x * 2 + c, (t + k) % 4))
    for cp in locals_:
        cp.wait()
    for k in zi:
        zz = (z - k + 8) % 8
        arrived(zi[k], KV.at[zz // 4, y, x, c, pl.ds(pl.multiple_of((zz % 4) * 32, 32), 32)])
    arrived(ri, RG.at[0, 0, 1 - zh])
    spare = pltpu.make_async_copy(RG.at[0, 0], RG.at[1, 0], lsem.at[2])
    spare.start()
    routes_sent = []
    for p, k in ((1, 1), (2, 3), (3, 2)):
        g = RG.at[0, 0]
        routes_sent.append((send(g, RG.at[0, p], dev(z, y, x + k, c)), RG.at[0, p]))
        routes_sent.append((send(g, RG.at[1, p], dev(z, y + k, x, c)), RG.at[1, p]))
    lo, hi = pl.ds(0, 64), pl.ds(64, 64)
    xm, xp, xo = (x + 3) % 4, (x + 1) % 4, (x + 2) % 4
    ym, yp, yo = (y + 3) % 4, (y + 1) % 4, (y + 2) % 4
    a, b = KV.at[0, y, x, c], KV.at[1, y, x, c]
    ap = send(a, a, xs[0])
    am = send(a, a, xs[1])
    bp = send(b, b, ys[0])
    bm = send(b, b, ys[1])
    arrived(ap, KV.at[0, y, xm, c])
    g = KV.at[0, y, xm, c, lo]
    ap2 = send(g, g, xs[0])
    arrived(bp, KV.at[1, ym, x, c])
    g = KV.at[1, ym, x, c, lo]
    bp2 = send(g, g, ys[0])
    arrived(am, KV.at[0, y, xp, c])
    g = KV.at[0, y, xp, c, hi]
    am2 = send(g, g, xs[1])
    arrived(bm, KV.at[1, yp, x, c])
    g = KV.at[1, yp, x, c, hi]
    bm2 = send(g, g, ys[1])
    arrived(ap2, KV.at[0, y, xo, c, lo])
    arrived(am2, KV.at[0, y, xo, c, hi])
    r = KV.at[0, y, :, c]
    rp = send(r, r, ys[0])
    rm = send(r, r, ys[1])
    arrived(bp2, KV.at[1, yo, x, c, lo])
    arrived(bm2, KV.at[1, yo, x, c, hi])
    q = KV.at[1, :, x, c]
    qp = send(q, q, xs[0])
    qm = send(q, q, xs[1])
    across = [send(r, r, other), send(q, q, other)]
    for k in ti:
        arrived(ti[k], NT.at[(t - k + 4) % 4])
    queries = jnp.dot(
        NT[...].reshape(128, 2048), qw_ref[...], preferred_element_type=F32
    ).T.astype(BF)
    lane = lax.broadcasted_iota(jnp.int32, (576, 128), 1)
    for pair in (0, 1):
        heads = []
        for h in (2 * pair, 2 * pair + 1):
            at = h * 192
            long = jnp.dot(uk_ref[h], queries[at : at + 128], preferred_element_type=F32)
            one = queries[at + 128 : at + 160].astype(F32)
            two = queries[at + 160 : at + 192].astype(F32)
            turned = [one * cos_ref[...] - two * sin_ref[...],
                      two * cos_ref[...] + one * sin_ref[...]]
            heads.append(jnp.concatenate([long] + turned, axis=0))
        cols = pl.ds(pair * 128, 128)
        QO[0, 0:576, cols] = jnp.where(lane < 64, heads[0], pltpu.roll(heads[1], 64, 1)).astype(BF)
        QO[1, 0:576, cols] = jnp.where(lane < 64, pltpu.roll(heads[0], 64, 1), heads[1]).astype(BF)
    QO[:, 576:640, :] = jnp.zeros((2, 64, 256), BF)
    arrived(rp, KV.at[0, ym, :, c])
    g = KV.at[0, ym, :, c, lo]
    rp2 = send(g, g, ys[0])
    arrived(qp, KV.at[1, :, xm, c])
    g = KV.at[1, :, xm, c, lo]
    qp2 = send(g, g, xs[0])
    arrived(rm, KV.at[0, yp, :, c])
    g = KV.at[0, yp, :, c, hi]
    rm2 = send(g, g, ys[1])
    arrived(qm, KV.at[1, :, xp, c])
    g = KV.at[1, :, xp, c, hi]
    qm2 = send(g, g, xs[1])
    for g in (KV.at[0, ym, :, c], KV.at[1, :, xm, c], KV.at[0, yp, :, c], KV.at[1, :, xp, c]):
        across.append(send(g, g, other))
    arrived(rp2, KV.at[0, yo, :, c, lo])
    arrived(rm2, KV.at[0, yo, :, c, hi])
    g = KV.at[0, yo, :, c]
    across.append(send(g, g, other))
    arrived(qp2, KV.at[1, :, xo, c, lo])
    arrived(qm2, KV.at[1, :, xo, c, hi])
    g = KV.at[1, :, xo, c]
    across.append(send(g, g, other))
    d = 1 - c
    for i, region in zip(
        across,
        (
            KV.at[0, y, :, d],
            KV.at[1, :, x, d],
            KV.at[0, ym, :, d],
            KV.at[1, :, xm, d],
            KV.at[0, yp, :, d],
            KV.at[1, :, xp, d],
            KV.at[0, yo, :, d],
            KV.at[1, :, xo, d],
        ),
    ):
        arrived(i, region)
    spare.wait()
    for i, region in routes_sent:
        arrived(i, region)
    for cp in sent:
        cp.wait_send()


def gather_keys(kv_own, normed_own, rg, qw, uk, cosine, sine):
    count = 48
    vm = pl.BlockSpec(memory_space=pltpu.VMEM)
    return pl.pallas_call(
        gather_kernel,
        out_shape=(
            jax.ShapeDtypeStruct((2, 4, 4, 2, 128, KEYW), BF),
            jax.ShapeDtypeStruct((2, KEYW, 256), BF),
            jax.ShapeDtypeStruct((2, 4, 2, 4, 16, 32), F32),
        ),
        in_specs=[vm] * 7,
        out_specs=(pl.BlockSpec(memory_space=pltpu.HBM), vm, vm),
        scratch_shapes=[
            pltpu.VMEM((4, 32, 2048), BF),
            pltpu.SemaphoreType.DMA((count,)),
            pltpu.SemaphoreType.DMA((count,)),
            pltpu.SemaphoreType.DMA((3,)),
        ],
        compiler_params=pltpu.CompilerParams(
            collective_id=0, has_side_effects=True, vmem_limit_bytes=60 * 2**20
        ),
        name="gather_keys",
    )(kv_own, normed_own, rg, qw, uk, cosine, sine)


CHUNK = 1024


def attention_kernel(inv_ref, blk_ref, q_ref, kv_hbm, o_ref, kbuf, m_ref, l_ref, acc_ref, sems):
    low = blk_ref[0]
    per = CHUNK // 64
    top_chunks = (127 - low) // per + 1

    def issue(p, carry):
        second = p >= 64
        d = inv_ref[jnp.where(second, 127 - p, p)]
        off = pl.multiple_of(jnp.where(second, 64, 0), 64)
        pltpu.make_async_copy(
            kv_hbm.at[d, pl.ds(off, 64)],
            kbuf.at[pl.ds(pl.multiple_of(p * 64, 64), 64)],
            sems.at[p // per],
        ).start()
        return carry

    lax.fori_loop(0, top_chunks * per, issue, 0)
    scale = (128 + 64) ** (-0.5)

    for half in (1, 0):
        block = low if half == 0 else 127 - low
        last = block // per
        m_ref[...] = jnp.full_like(m_ref, -1e30)
        l_ref[...] = jnp.zeros_like(l_ref)
        acc_ref[...] = jnp.zeros_like(acc_ref)

        def step(ch, masked):
            region = kbuf.at[pl.ds(pl.multiple_of(ch * CHUNK, CHUNK), CHUNK)]
            if half == 1:
                pltpu.make_async_copy(region, region, sems.at[ch]).wait()
            keys = region[...]
            s = jnp.dot(keys, q_ref[half], preferred_element_type=F32) * scale
            if masked:
                key = lax.broadcasted_iota(jnp.int32, s.shape, 0)
                query = lax.broadcasted_iota(jnp.int32, s.shape, 1) % 64
                s = jnp.where(key - query <= block * 64 - ch * CHUNK, s, -1e30)
            m_old = m_ref[...]
            m_new = jnp.maximum(m_old, jnp.max(s, axis=0, keepdims=True))
            p = jnp.exp(s - m_new)
            alpha = jnp.exp(m_old - m_new)
            l_ref[...] = l_ref[...] * alpha + jnp.sum(p, axis=0, keepdims=True)
            m_ref[...] = m_new
            acc_ref[...] = acc_ref[...] * alpha + lax.dot_general(
                keys[:, :512], p.astype(BF), (((0,), (0,)), ((), ())), preferred_element_type=F32
            )

        def loop(ch, carry):
            step(ch, False)
            return carry

        lax.fori_loop(0, last, loop, 0)
        step(last, True)
        o_ref[half] = (acc_ref[...] / l_ref[...]).T.astype(BF)


def attention(inv, low, q, kv):
    return pl.pallas_call(
        attention_kernel,
        out_shape=jax.ShapeDtypeStruct((2, 256, 512), BF),
        in_specs=[
            pl.BlockSpec(memory_space=pltpu.SMEM),
            pl.BlockSpec(memory_space=pltpu.SMEM),
            pl.BlockSpec(memory_space=pltpu.VMEM),
            pl.BlockSpec(memory_space=pltpu.HBM),
        ],
        out_specs=pl.BlockSpec(memory_space=pltpu.VMEM),
        scratch_shapes=[
            pltpu.VMEM((8192, KEYW), BF),
            pltpu.VMEM((1, 256), F32),
            pltpu.VMEM((1, 256), F32),
            pltpu.VMEM((512, 256), F32),
            pltpu.SemaphoreType.DMA((8192 // CHUNK,)),
        ],
        compiler_params=pltpu.CompilerParams(vmem_limit_bytes=60 * 2**20),
        name="attention",
    )(inv, low, q, kv)


def tp_scatter_kernel(p_ref, o_ref, ssem, rsem, lsem):
    z, y, x, c = place()
    s, t = lax.axis_index("seq"), lax.axis_index("tp")
    greet([(s, (t + k) % 4) for k in (1, 2, 3)])
    cps = []
    for k in (2, 3, 1):
        to = (t + k) % 4
        cp = rcopy(p_ref.at[to], o_ref.at[k], ssem.at[k], rsem.at[k], (s, to))
        cp.start()
        cps.append(cp)
    own = pltpu.make_async_copy(p_ref.at[t], o_ref.at[0], lsem)
    own.start()
    own.wait()
    for cp in cps:
        cp.wait()


def exchange(kernel, name, cid, array, out):
    vm = pl.BlockSpec(memory_space=pltpu.VMEM)
    return pl.pallas_call(
        kernel,
        out_shape=jax.ShapeDtypeStruct(out, BF),
        in_specs=[vm],
        out_specs=vm,
        scratch_shapes=[
            pltpu.SemaphoreType.DMA((8,)),
            pltpu.SemaphoreType.DMA((8,)),
            pltpu.SemaphoreType.DMA,
        ],
        compiler_params=pltpu.CompilerParams(
            collective_id=cid, has_side_effects=True, vmem_limit_bytes=16 * 2**20
        ),
        name=name,
    )(array)


def experts_kernel(
    own, slots, gates, wg, wu, wd, out,
    X, S, R, O, M, T, rbuf, sbuf, home, H, Qs, Q,
    sx, rx, sz, rz, s2, r2, s3, r3, sr, rr, s4, r4, sf, rf, sq, rq, lsem,
):
    z, y, x, c = place()
    towards = [dev(z + 1, y, x, c), dev(z + 7, y, x, c)]
    peers = towards + [dev(z, y, x, c + 1)]
    for k in (1, 2, 3):
        for d in (0, 1):
            peers.append(dev(z, y + k, x, c + d))
            peers.append(dev(z, y, x + k, c + d))
    greet(peers)
    odd = z % 2

    def first(p, k):
        return rcopy(
            own, X.at[z, p], sx.at[p], rx.at[p], dev(z, y + k * odd, x + k * (1 - odd), c)
        )

    def opposite(r):
        o = (z + r) % 2
        return dev(z, y + 2 * o, x + 2 * (1 - o), c)

    for p, k in ((1, 1), (2, 3)):
        first(p, k).start()
    here = pltpu.make_async_copy(own, X.at[z, 0], lsem)
    here.start()

    def shard(d, s):
        return (z + 8 - s) % 8 if d == 0 else (z + s) % 8

    def ring(d, s, h):
        part = X.at[shard(d, s - 1), pl.ds(0, 3), pl.ds(16 * h, 16)]
        return rcopy(part, part, sz.at[d, s - 1, h], rz.at[d, s - 1, h], towards[d])

    def fourth(r):
        u = (z + r) % 8
        return rcopy(X.at[u, 0], X.at[u, 3], sf.at[r], rf.at[r], opposite(r))

    here.wait()
    first(1, 1).wait_recv()
    first(2, 3).wait_recv()
    for h in (0, 1):
        for d in (0, 1):
            ring(d, 1, h).start()
    fourth(0).start()

    def rows16(j):
        return pl.ds(j * 16, 16)

    def partner(r, j, sign):
        o = (z + r) % 2
        step = (j // 2) * sign + 4
        return dev(z, y + step * (1 - o), x + step * o, c + j % 2)

    def hop2(r, j):
        return rcopy(
            S.at[r, rows16(j)], R.at[r, rows16(j)], s2.at[r, j], r2.at[r, j], partner(r, j, 1)
        )

    def hop3(r, j):
        return rcopy(
            O.at[r, rows16(j)], M.at[r, rows16(j)], s3.at[r, j], r3.at[r, j], partner(r, j, -1)
        )

    number = lax.broadcasted_iota(jnp.int32, (8, 16, 32), 1).astype(F32)

    def table(r, scale=None):
        u = (z + r) % 8
        parts = []
        for p in range(4):
            part = (slots[u, p][:, None, :] == number).astype(F32)
            if scale is not None:
                part = part * scale[u, p][:, None, :]
            parts.append(part.reshape(128, 32))
        return jnp.concatenate(parts, axis=1)

    def spread(r):
        tokens = X[(z + r) % 8].reshape(128, 2048)
        S[r] = jnp.dot(
            table(r).astype(BF), tokens, preferred_element_type=F32
        ).astype(BF)
        for j in (4, 5, 2, 6, 3, 7, 1):
            hop2(r, j).start()
        R[r, 0:16] = S[r, 0:16]

    def across(rows, weight):
        return lax.dot_general(
            rows, weight[...], (((1,), (1,)), ((), ())), preferred_element_type=F32
        )

    def work(ra, rb):
        for r in (ra, rb):
            for j in range(1, 8):
                hop2(r, j).wait_recv()
        rows = jnp.concatenate([R[ra], R[rb]], axis=0)
        gate = across(rows, wg)
        up = across(rows, wu)
        hidden = (gate / (1.0 + jnp.exp(-gate)) * up).astype(BF)
        result = jnp.dot(hidden, wd[...], preferred_element_type=F32).astype(BF)
        O[ra] = result[:128]
        O[rb] = result[128:]
        M[ra, 0:16] = result[0:16]
        M[rb, 0:16] = result[128:144]
        for r in (ra, rb):
            for j in (4, 5, 2, 6, 3, 7, 1):
                hop3(r, j).start()

    def pass_on(s, h):
        for d in (0, 1):

            @pl.when((s < 4) | ((s == 4) & (h == d)))
            def _():
                part = X.at[shard(d, s), pl.ds(0, 3), pl.ds(16 * h, 16)]
                rcopy(part, part, sz.at[d, s - 1, h], rz.at[d, s - 1, h], towards[d]).wait_recv()

            @pl.when((s < 3) | ((s == 3) & (h == d)))
            def _():
                ring(d, s + 1, h).start()

    def step(s, carry):
        @pl.when(s < 5)
        def _():
            pass_on(s, 0)

        @pl.when(s < 6)
        def _():
            fourth((9 - s) % 8).wait_recv()
            spread((9 - s) % 8)

        @pl.when((s > 1) & (s < 5))
        def _():
            fourth(s - 1).wait_recv()
            spread(s - 1)

        @pl.when(s < 5)
        def _():
            pass_on(s, 1)
            fourth((8 - s) % 8).start()

        @pl.when(s < 4)
        def _():
            fourth(s).start()

        @pl.when(s > 2)
        def _():
            work((11 - s) % 8, s - 2)

        return carry

    lax.fori_loop(1, 7, step, 0)

    def quarter(r):
        return rcopy(Qs.at[r], Q.at[r], sq.at[r], rq.at[r], opposite(r))

    def weigh(r):
        for j in range(1, 8):
            hop3(r, j).wait_recv()
        w = table(r, gates)
        hi = w.astype(BF)
        lo = (w - hi.astype(F32)).astype(BF)
        dims = (((0,), (0,)), ((), ()))
        sums = lax.dot_general(hi, M[r], dims, preferred_element_type=F32) + lax.dot_general(
            lo, M[r], dims, preferred_element_type=F32
        )
        Qs[r] = sums[96:].astype(BF)
        T[r] = sums[:96]
        quarter(r).start()

    def joined(r):
        quarter(r).wait_recv()
        T[r, 0:32] = T[r, 0:32] + Q[r].astype(F32)

    def half(h):
        return pl.ds(h * 48, 48)

    def reduce(d, s, h):
        return rcopy(
            sbuf.at[d, s - 1, half(h)], rbuf.at[d, s - 1, half(h)],
            sr.at[d, s - 1, h], rr.at[d, s - 1, h], towards[d],
        )

    weigh(4)
    weigh(5)
    weigh(3)
    joined(4)
    for d in (0, 1):
        sbuf[d, 0, half(d)] = T[4, half(d)].astype(BF)
    for d in (0, 1):
        reduce(d, 1, d).start()

    def fold(s, carry):
        joined(5 - s)
        joined(3 + s)
        for h in (0, 1):
            for d, r in ((0, 5 - s), (1, 3 + s)):

                @pl.when((s > 2) | (h == d))
                def _():
                    reduce(d, s - 1, h).wait_recv()
                    sbuf[d, s - 1, half(h)] = (
                        T[r, half(h)] + rbuf[d, s - 2, half(h)].astype(F32)
                    ).astype(BF)

                @pl.when((s == 2) & (h != d))
                def _():
                    sbuf[d, s - 1, half(h)] = T[r, half(h)].astype(BF)

            for d in (0, 1):
                reduce(d, s, h).start()
        weigh(4 - s)

        @pl.when(s < 4)
        def _():
            weigh(4 + s)

        return carry

    lax.fori_loop(2, 5, fold, 0)
    joined(0)
    for h in (0, 1):
        for d in (0, 1):
            reduce(d, 4, h).wait_recv()
    T[0] = T[0] + rbuf[0, 3].astype(F32) + rbuf[1, 3].astype(F32)
    home[...] = T[0].astype(BF)

    def last(p, k):
        return rcopy(
            home.at[pl.ds(p * 32, 32)], H.at[p], s4.at[p], r4.at[p],
            dev(z, y + (4 - k) * odd, x + (4 - k) * (1 - odd), c),
        )

    total = T[0, 0:32]
    for p, k in ((1, 1), (2, 3)):
        last(p, k).start()
    for p, k in ((1, 1), (2, 3)):
        last(p, k).wait_recv()
        total += H[p].astype(F32)
    out[...] = total

    for p, k in ((1, 1), (2, 3)):
        first(p, k).wait_send()
        last(p, k).wait_send()
    for d in (0, 1):
        for s in (1, 2, 3, 4):
            for h in (0, 1):
                if s < 4 or h == d:
                    ring(d, s, h).wait_send()
                if s > 1 or h == d:
                    reduce(d, s, h).wait_send()

    def drain(r, carry):
        fourth(r).wait_send()
        quarter(r).wait_send()
        for j in range(1, 8):
            hop2(r, j).wait_send()
            hop3(r, j).wait_send()
        return carry

    lax.fori_loop(0, 8, drain, 0)


def experts(own, slots, gates, wg, wu, wd):
    vm = pl.BlockSpec(memory_space=pltpu.VMEM)
    big = pltpu.VMEM((8, 128, 2048), BF)
    dma = pltpu.SemaphoreType.DMA
    return pl.pallas_call(
        experts_kernel,
        out_shape=jax.ShapeDtypeStruct((32, 2048), F32),
        in_specs=[vm] * 6,
        out_specs=vm,
        scratch_shapes=[
            pltpu.VMEM((8, 4, 32, 2048), BF), big, big, big, big,
            pltpu.VMEM((8, 96, 2048), F32),
            pltpu.VMEM((2, 4, 96, 2048), BF),
            pltpu.VMEM((2, 4, 96, 2048), BF),
            pltpu.VMEM((96, 2048), BF),
            pltpu.VMEM((3, 32, 2048), BF),
            pltpu.VMEM((8, 32, 2048), BF),
            pltpu.VMEM((8, 32, 2048), BF),
            dma((4,)), dma((4,)),
            dma((2, 4, 2)), dma((2, 4, 2)),
            dma((8, 8)), dma((8, 8)), dma((8, 8)), dma((8, 8)),
            dma((2, 4, 2)), dma((2, 4, 2)),
            dma((4,)), dma((4,)),
            dma((8,)), dma((8,)), dma((8,)), dma((8,)),
            dma,
        ],
        compiler_params=pltpu.CompilerParams(
            collective_id=4, has_side_effects=True, vmem_limit_bytes=60 * 2**20
        ),
        name="experts",
    )(own, slots, gates, wg, wu, wd)


def slot_tables(rgs, z, y, x, c):
    plane = lax.broadcasted_iota(jnp.int32, (4, 2, 4, 16, 32), 2)
    mine = jnp.where(plane % 2 == 0, rgs[0], rgs[1])
    mine = mine.transpose(1, 2, 0, 3, 4).reshape(8, 4, 16, 32)
    routes = mine[:, :, :6].astype(jnp.int32)
    gates = mine[:, :, 8:14]
    off = jnp.arange(8, dtype=jnp.int32) // 2
    core = (c + jnp.arange(8, dtype=jnp.int32) % 2) % 2
    base = (z // 4) * 32
    along_y = base + ((y + off) % 4) * 8 + x * 2 + core
    along_x = base + y * 8 + ((x + off) % 4) * 2 + core
    u = jnp.arange(8, dtype=jnp.int32)[:, None]
    expert = jnp.where(u % 2 == 0, along_y[None], along_x[None])
    hit = routes[:, :, None] == expert[:, None, :, None, None]
    member = jnp.any(hit, axis=3)
    gate = jnp.sum(jnp.where(hit, gates[:, :, None], 0.0), axis=3)
    ti = lax.broadcasted_iota(jnp.int32, (32, 32), 0)
    tj = lax.broadcasted_iota(jnp.int32, (32, 32), 1)
    before = (ti < tj).astype(BF)
    rank = jnp.dot(
        member.astype(BF).reshape(256, 32), before, preferred_element_type=F32
    ).reshape(8, 4, 8, 32)
    place_ = lax.broadcasted_iota(jnp.int32, (8, 4, 8, 32), 1)
    slot = jnp.where(member, (place_ * 4).astype(F32) + rank, -1.0)
    return slot, gate


def body(
    tokens, block_ids, attn_gain, q_weight, kv_weight, kv_gain, uk_weight, uv_weight,
    o_weight, ffn_gain, w_gate, w_up, w_down, routes, gate_weights,
):
    z, y, x, c = place()
    t = lax.axis_index("tp")
    s = lax.axis_index("seq")
    own_blocks = lax.dynamic_slice(block_ids, (s, 0), (1, 2))[0]
    normed_own = normalize(tokens, attn_gain).astype(BF)
    own_pos = own_blocks[t // 2] * 64 + (t % 2) * 32 + jnp.arange(32, dtype=jnp.int32)
    projected = jnp.dot(normed_own, kv_weight, preferred_element_type=F32)
    latent = normalize(projected[:, :512], kv_gain).astype(BF)
    key_rope = rotate(projected[:, 512:], own_pos).astype(BF)
    kv_own = jnp.concatenate([latent, key_rope, jnp.zeros((32, 64), BF)], axis=1)
    pad2 = jnp.zeros((4, 32, 2), F32)
    rg = jnp.concatenate(
        [
            routes.astype(F32).reshape(4, 32, 6), pad2,
            gate_weights.reshape(4, 32, 6), pad2,
        ],
        axis=2,
    ).transpose(0, 2, 1)
    query_pos = (own_blocks[:, None] * 64 + jnp.arange(64, dtype=jnp.int32)[None, :]).reshape(128)
    frequency = jnp.exp(jnp.arange(32, dtype=F32) * (-2.0 * math.log(10000.0) / 64))
    angles = frequency[:, None] * query_pos.astype(F32)[None, :]
    kv, q, rgs = gather_keys(
        kv_own, normed_own, rg, q_weight, uk_weight, jnp.cos(angles), jnp.sin(angles)
    )
    ids = jnp.arange(64, dtype=jnp.int32)
    inv = jnp.sum(
        jnp.where(block_ids[:, 0][None, :] == ids[:, None], ids[None, :], 0), axis=1
    ).astype(jnp.int32)
    out_latent = attention(inv, own_blocks[:1], q, kv.reshape(64, 128, KEYW))
    out_latent = out_latent.reshape(2, 4, 64, 512).transpose(1, 0, 2, 3).reshape(4, 128, 512)
    head_out = jnp.einsum(
        "htl,hlv->thv", out_latent, uv_weight, preferred_element_type=F32
    ).astype(BF)
    partial_out = jnp.dot(head_out.reshape(128, 512), o_weight, preferred_element_type=F32)
    parts = exchange(
        tp_scatter_kernel, "tp_scatter", 1, partial_out.astype(BF).reshape(4, 32, 2048),
        (4, 32, 2048),
    )
    attn_own = jnp.sum(parts.astype(F32), axis=0)
    mixed = (tokens.astype(F32) + attn_own).astype(BF)
    normed_ffn = normalize(mixed, ffn_gain).astype(BF)
    slots, gates = slot_tables(rgs, z, y, x, c)
    sums = experts(normed_ffn, slots, gates, w_gate[0].T, w_up[0].T, w_down[0])
    return (mixed.astype(F32) + sums).astype(BF)


def solution(mesh):
    return jax.shard_map(
        body,
        mesh=mesh,
        in_specs=(
            P(("seq", "tp"), None), P(), P(), P(None, "tp"), P(), P(),
            P("tp", None, None), P("tp", None, None), P("tp", None), P(),
            P("seq", None, "tp"), P("seq", None, "tp"), P("seq", "tp", None),
            P("seq", None), P("seq", None),
        ),
        out_specs=P(("seq", "tp"), None),
        check_vma=False,
    )
```

```python
import functools
import math

import jax
import jax.numpy as jnp
from jax import lax
from jax.experimental import pallas as pl
from jax.experimental.pallas import tpu as pltpu
from jax.sharding import PartitionSpec as P

EPSILON = 1e-06
MESH = pl.DeviceIdType.MESH
BF = jnp.bfloat16
F32 = jnp.float32
KEYW = 640


def place():
    s = lax.axis_index("seq")
    t = lax.axis_index("tp")
    return (s // 32) * 4 + t, (s // 8) % 4, (s // 2) % 4, s % 2


def dev(z, y, x, c):
    z, y, x, c = z % 8, y % 4, x % 4, c % 2
    return ((z // 4) * 32 + y * 8 + x * 2 + c, z % 4)


def greet(peers):
    barrier = pltpu.get_barrier_semaphore()
    for p in peers:
        pl.semaphore_signal(barrier, inc=1, device_id=p, device_id_type=MESH)
    pl.semaphore_wait(barrier, len(peers))


def rcopy(src, dst, ss, rs, device):
    return pltpu.make_async_remote_copy(
        src_ref=src, dst_ref=dst, send_sem=ss, recv_sem=rs, device_id=device, device_id_type=MESH
    )


def normalize(values, gain_vec):
    values = values.astype(F32)
    factor = lax.rsqrt(jnp.mean(values * values, axis=-1, keepdims=True) + EPSILON)
    return values * factor * gain_vec


def rotate(values, position):
    half_width = values.shape[-1] // 2
    frequency = jnp.exp(
        jnp.arange(half_width, dtype=F32) * (-2.0 * math.log(10000.0) / values.shape[-1])
    )
    angles = position.astype(F32).reshape(position.shape + (1,) * (values.ndim - 1)) * frequency
    cosine = jnp.cos(angles)
    sine_part = jnp.sin(angles)
    first_half = values[..., :half_width]
    second_half = values[..., half_width:]
    return jnp.concatenate(
        [
            first_half * cosine - second_half * sine_part,
            second_half * cosine + first_half * sine_part,
        ],
        axis=-1,
    )


def gather_kernel(
    kv_ref, nt_ref, rg_ref, qw_ref, uk_ref, cos_ref, sin_ref, KV, QO, RG, NT, ssem, rsem, lsem
):
    z, y, x, c = place()
    zh, t = z // 4, z % 4
    peers = [dev(z + k, y, x, c) for k in range(1, 8)]
    xs = [dev(z, y, x + 1, c), dev(z, y, x + 3, c), dev(z, y, x + 2, c)]
    ys = [dev(z, y + 1, x, c), dev(z, y + 3, x, c), dev(z, y + 2, x, c)]
    other = dev(z, y, x, c + 1)
    greet(peers + xs + ys + [other])
    number = [0]
    sent = []

    def send(src, dst, device):
        i = number[0]
        number[0] += 1
        cp = rcopy(src, dst, ssem.at[i], rsem.at[i], device)
        cp.start()
        sent.append(cp)
        return i

    def arrived(i, region):
        rcopy(region, region, ssem.at[i], rsem.at[i], other).wait_recv()

    rows = pl.ds(pl.multiple_of(t * 32, 32), 32)
    zi = {}
    mine = KV.at[zh, y, x, c, rows]
    for k in (4, 3, 5, 2, 6, 1, 7):
        zi[k] = send(kv_ref, mine, dev(z + k, y, x, c))
    locals_ = [
        pltpu.make_async_copy(kv_ref, mine, lsem.at[0]),
        pltpu.make_async_copy(nt_ref, NT.at[t], lsem.at[1]),
        pltpu.make_async_copy(rg_ref, RG.at[0, 0, zh], lsem.at[2]),
    ]
    for cp in locals_:
        cp.start()
    ri = send(rg_ref, RG.at[0, 0, zh], dev(z + 4, y, x, c))
    ti = {}
    for k in (3, 2, 1):
        ti[k] = send(nt_ref, NT.at[t], (zh * 32 + y * 8 + x * 2 + c, (t + k) % 4))
    for cp in locals_:
        cp.wait()
    for k in zi:
        zz = (z - k + 8) % 8
        arrived(zi[k], KV.at[zz // 4, y, x, c, pl.ds(pl.multiple_of((zz % 4) * 32, 32), 32)])
    arrived(ri, RG.at[0, 0, 1 - zh])
    spare = pltpu.make_async_copy(RG.at[0, 0], RG.at[1, 0], lsem.at[2])
    spare.start()
    routes_sent = []
    for p, k in ((1, 1), (2, 3), (3, 2)):
        g = RG.at[0, 0]
        routes_sent.append((send(g, RG.at[0, p], dev(z, y, x + k, c)), RG.at[0, p]))
        routes_sent.append((send(g, RG.at[1, p], dev(z, y + k, x, c)), RG.at[1, p]))
    lo, hi = pl.ds(0, 64), pl.ds(64, 64)
    xm, xp, xo = (x + 3) % 4, (x + 1) % 4, (x + 2) % 4
    ym, yp, yo = (y + 3) % 4, (y + 1) % 4, (y + 2) % 4
    a, b = KV.at[0, y, x, c], KV.at[1, y, x, c]
    ap = send(a, a, xs[0])
    am = send(a, a, xs[1])
    bp = send(b, b, ys[0])
    bm = send(b, b, ys[1])
    arrived(ap, KV.at[0, y, xm, c])
    g = KV.at[0, y, xm, c, lo]
    ap2 = send(g, g, xs[0])
    arrived(bp, KV.at[1, ym, x, c])
    g = KV.at[1, ym, x, c, lo]
    bp2 = send(g, g, ys[0])
    arrived(am, KV.at[0, y, xp, c])
    g = KV.at[0, y, xp, c, hi]
    am2 = send(g, g, xs[1])
    arrived(bm, KV.at[1, yp, x, c])
    g = KV.at[1, yp, x, c, hi]
    bm2 = send(g, g, ys[1])
    arrived(ap2, KV.at[0, y, xo, c, lo])
    arrived(am2, KV.at[0, y, xo, c, hi])
    r = KV.at[0, y, :, c]
    rp = send(r, r, ys[0])
    rm = send(r, r, ys[1])
    arrived(bp2, KV.at[1, yo, x, c, lo])
    arrived(bm2, KV.at[1, yo, x, c, hi])
    q = KV.at[1, :, x, c]
    qp = send(q, q, xs[0])
    qm = send(q, q, xs[1])
    across = [send(r, r, other), send(q, q, other)]
    for k in ti:
        arrived(ti[k], NT.at[(t - k + 4) % 4])
    queries = jnp.dot(
        NT[...].reshape(128, 2048), qw_ref[...], preferred_element_type=F32
    ).T.astype(BF)
    lane = lax.broadcasted_iota(jnp.int32, (576, 128), 1)
    for pair in (0, 1):
        heads = []
        for h in (2 * pair, 2 * pair + 1):
            at = h * 192
            long = jnp.dot(uk_ref[h], queries[at : at + 128], preferred_element_type=F32)
            one = queries[at + 128 : at + 160].astype(F32)
            two = queries[at + 160 : at + 192].astype(F32)
            turned = [one * cos_ref[...] - two * sin_ref[...],
                      two * cos_ref[...] + one * sin_ref[...]]
            heads.append(jnp.concatenate([long] + turned, axis=0))
        cols = pl.ds(pair * 128, 128)
        QO[0, 0:576, cols] = jnp.where(lane < 64, heads[0], pltpu.roll(heads[1], 64, 1)).astype(BF)
        QO[1, 0:576, cols] = jnp.where(lane < 64, pltpu.roll(heads[0], 64, 1), heads[1]).astype(BF)
    QO[:, 576:640, :] = jnp.zeros((2, 64, 256), BF)
    arrived(rp, KV.at[0, ym, :, c])
    g = KV.at[0, ym, :, c, lo]
    rp2 = send(g, g, ys[0])
    arrived(qp, KV.at[1, :, xm, c])
    g = KV.at[1, :, xm, c, lo]
    qp2 = send(g, g, xs[0])
    arrived(rm, KV.at[0, yp, :, c])
    g = KV.at[0, yp, :, c, hi]
    rm2 = send(g, g, ys[1])
    arrived(qm, KV.at[1, :, xp, c])
    g = KV.at[1, :, xp, c, hi]
    qm2 = send(g, g, xs[1])
    for g in (KV.at[0, ym, :, c], KV.at[1, :, xm, c], KV.at[0, yp, :, c], KV.at[1, :, xp, c]):
        across.append(send(g, g, other))
    arrived(rp2, KV.at[0, yo, :, c, lo])
    arrived(rm2, KV.at[0, yo, :, c, hi])
    g = KV.at[0, yo, :, c]
    across.append(send(g, g, other))
    arrived(qp2, KV.at[1, :, xo, c, lo])
    arrived(qm2, KV.at[1, :, xo, c, hi])
    g = KV.at[1, :, xo, c]
    across.append(send(g, g, other))
    d = 1 - c
    for i, region in zip(
        across,
        (
            KV.at[0, y, :, d],
            KV.at[1, :, x, d],
            KV.at[0, ym, :, d],
            KV.at[1, :, xm, d],
            KV.at[0, yp, :, d],
            KV.at[1, :, xp, d],
            KV.at[0, yo, :, d],
            KV.at[1, :, xo, d],
        ),
    ):
        arrived(i, region)
    spare.wait()
    for i, region in routes_sent:
        arrived(i, region)
    for cp in sent:
        cp.wait_send()


def gather_keys(kv_own, normed_own, rg, qw, uk, cosine, sine):
    count = 48
    vm = pl.BlockSpec(memory_space=pltpu.VMEM)
    return pl.pallas_call(
        gather_kernel,
        out_shape=(
            jax.ShapeDtypeStruct((2, 4, 4, 2, 128, KEYW), BF),
            jax.ShapeDtypeStruct((2, KEYW, 256), BF),
            jax.ShapeDtypeStruct((2, 4, 2, 4, 16, 32), F32),
        ),
        in_specs=[vm] * 7,
        out_specs=(pl.BlockSpec(memory_space=pltpu.HBM), vm, vm),
        scratch_shapes=[
            pltpu.VMEM((4, 32, 2048), BF),
            pltpu.SemaphoreType.DMA((count,)),
            pltpu.SemaphoreType.DMA((count,)),
            pltpu.SemaphoreType.DMA((3,)),
        ],
        compiler_params=pltpu.CompilerParams(
            collective_id=0, has_side_effects=True, vmem_limit_bytes=60 * 2**20
        ),
        name="gather_keys",
    )(kv_own, normed_own, rg, qw, uk, cosine, sine)


CHUNK = 1024


def attention_kernel(inv_ref, blk_ref, q_ref, kv_hbm, o_ref, kbuf, m_ref, l_ref, acc_ref, sems):
    low = blk_ref[0]
    per = CHUNK // 64
    top_chunks = (127 - low) // per + 1

    def issue(p, carry):
        second = p >= 64
        d = inv_ref[jnp.where(second, 127 - p, p)]
        off = pl.multiple_of(jnp.where(second, 64, 0), 64)
        pltpu.make_async_copy(
            kv_hbm.at[d, pl.ds(off, 64)],
            kbuf.at[pl.ds(pl.multiple_of(p * 64, 64), 64)],
            sems.at[p // per],
        ).start()
        return carry

    lax.fori_loop(0, top_chunks * per, issue, 0)
    scale = (128 + 64) ** (-0.5)

    for half in (1, 0):
        block = low if half == 0 else 127 - low
        last = block // per
        m_ref[...] = jnp.full_like(m_ref, -1e30)
        l_ref[...] = jnp.zeros_like(l_ref)
        acc_ref[...] = jnp.zeros_like(acc_ref)

        def step(ch, masked):
            region = kbuf.at[pl.ds(pl.multiple_of(ch * CHUNK, CHUNK), CHUNK)]
            if half == 1:
                pltpu.make_async_copy(region, region, sems.at[ch]).wait()
            keys = region[...]
            s = jnp.dot(keys, q_ref[half], preferred_element_type=F32) * scale
            if masked:
                key = lax.broadcasted_iota(jnp.int32, s.shape, 0)
                query = lax.broadcasted_iota(jnp.int32, s.shape, 1) % 64
                s = jnp.where(key - query <= block * 64 - ch * CHUNK, s, -1e30)
            m_old = m_ref[...]
            m_new = jnp.maximum(m_old, jnp.max(s, axis=0, keepdims=True))
            p = jnp.exp(s - m_new)
            alpha = jnp.exp(m_old - m_new)
            l_ref[...] = l_ref[...] * alpha + jnp.sum(p, axis=0, keepdims=True)
            m_ref[...] = m_new
            acc_ref[...] = acc_ref[...] * alpha + lax.dot_general(
                keys[:, :512], p.astype(BF), (((0,), (0,)), ((), ())), preferred_element_type=F32
            )

        def loop(ch, carry):
            step(ch, False)
            return carry

        lax.fori_loop(0, last, loop, 0)
        step(last, True)
        o_ref[half] = (acc_ref[...] / l_ref[...]).T.astype(BF)


def attention(inv, low, q, kv):
    return pl.pallas_call(
        attention_kernel,
        out_shape=jax.ShapeDtypeStruct((2, 256, 512), BF),
        in_specs=[
            pl.BlockSpec(memory_space=pltpu.SMEM),
            pl.BlockSpec(memory_space=pltpu.SMEM),
            pl.BlockSpec(memory_space=pltpu.VMEM),
            pl.BlockSpec(memory_space=pltpu.HBM),
        ],
        out_specs=pl.BlockSpec(memory_space=pltpu.VMEM),
        scratch_shapes=[
            pltpu.VMEM((8192, KEYW), BF),
            pltpu.VMEM((1, 256), F32),
            pltpu.VMEM((1, 256), F32),
            pltpu.VMEM((512, 256), F32),
            pltpu.SemaphoreType.DMA((8192 // CHUNK,)),
        ],
        compiler_params=pltpu.CompilerParams(vmem_limit_bytes=60 * 2**20),
        name="attention",
    )(inv, low, q, kv)


def tp_scatter_kernel(p_ref, o_ref, ssem, rsem, lsem):
    z, y, x, c = place()
    s, t = lax.axis_index("seq"), lax.axis_index("tp")
    greet([(s, (t + k) % 4) for k in (1, 2, 3)])
    cps = []
    for k in (2, 3, 1):
        to = (t + k) % 4
        cp = rcopy(p_ref.at[to], o_ref.at[k], ssem.at[k], rsem.at[k], (s, to))
        cp.start()
        cps.append(cp)
    own = pltpu.make_async_copy(p_ref.at[t], o_ref.at[0], lsem)
    own.start()
    own.wait()
    for cp in cps:
        cp.wait()


def exchange(kernel, name, cid, array, out):
    vm = pl.BlockSpec(memory_space=pltpu.VMEM)
    return pl.pallas_call(
        kernel,
        out_shape=jax.ShapeDtypeStruct(out, BF),
        in_specs=[vm],
        out_specs=vm,
        scratch_shapes=[
            pltpu.SemaphoreType.DMA((8,)),
            pltpu.SemaphoreType.DMA((8,)),
            pltpu.SemaphoreType.DMA,
        ],
        compiler_params=pltpu.CompilerParams(
            collective_id=cid, has_side_effects=True, vmem_limit_bytes=16 * 2**20
        ),
        name=name,
    )(array)


def experts_kernel(
    own, slots, gates, wg, wu, wd, out,
    X, S, R, O, M, T, rbuf, sbuf, home, H, Qs, Q,
    sx, rx, sz, rz, s2, r2, s3, r3, sr, rr, s4, r4, sf, rf, sq, rq, lsem,
):
    z, y, x, c = place()
    towards = [dev(z + 1, y, x, c), dev(z + 7, y, x, c)]
    peers = towards + [dev(z, y, x, c + 1)]
    for k in (1, 2, 3):
        for d in (0, 1):
            peers.append(dev(z, y + k, x, c + d))
            peers.append(dev(z, y, x + k, c + d))
    greet(peers)
    odd = z % 2

    def first(p, k):
        return rcopy(
            own, X.at[z, p], sx.at[p], rx.at[p], dev(z, y + k * odd, x + k * (1 - odd), c)
        )

    def opposite(r):
        o = (z + r) % 2
        return dev(z, y + 2 * o, x + 2 * (1 - o), c)

    for p, k in ((1, 1), (2, 3)):
        first(p, k).start()
    here = pltpu.make_async_copy(own, X.at[z, 0], lsem)
    here.start()

    def shard(d, s):
        return (z + 8 - s) % 8 if d == 0 else (z + s) % 8

    def ring(d, s, h):
        part = X.at[shard(d, s - 1), pl.ds(0, 3), pl.ds(16 * h, 16)]
        return rcopy(part, part, sz.at[d, s - 1, h], rz.at[d, s - 1, h], towards[d])

    def fourth(r):
        u = (z + r) % 8
        return rcopy(X.at[u, 0], X.at[u, 3], sf.at[r], rf.at[r], opposite(r))

    here.wait()
    first(1, 1).wait_recv()
    first(2, 3).wait_recv()
    for h in (0, 1):
        for d in (0, 1):
            ring(d, 1, h).start()
    fourth(0).start()

    def rows16(j):
        return pl.ds(j * 16, 16)

    def partner(r, j, sign):
        o = (z + r) % 2
        step = (j // 2) * sign + 4
        return dev(z, y + step * (1 - o), x + step * o, c + j % 2)

    def hop2(r, j):
        return rcopy(
            S.at[r, rows16(j)], R.at[r, rows16(j)], s2.at[r, j], r2.at[r, j], partner(r, j, 1)
        )

    def hop3(r, j):
        return rcopy(
            O.at[r, rows16(j)], M.at[r, rows16(j)], s3.at[r, j], r3.at[r, j], partner(r, j, -1)
        )

    number = lax.broadcasted_iota(jnp.int32, (8, 16, 32), 1).astype(F32)

    def table(r, scale=None):
        u = (z + r) % 8
        parts = []
        for p in range(4):
            part = (slots[u, p][:, None, :] == number).astype(F32)
            if scale is not None:
                part = part * scale[u, p][:, None, :]
            parts.append(part.reshape(128, 32))
        return jnp.concatenate(parts, axis=1)

    def spread(r):
        tokens = X[(z + r) % 8].reshape(128, 2048)
        S[r] = jnp.dot(
            table(r).astype(BF), tokens, preferred_element_type=F32
        ).astype(BF)
        for j in (4, 5, 2, 6, 3, 7, 1):
            hop2(r, j).start()
        R[r, 0:16] = S[r, 0:16]

    def across(rows, weight):
        return lax.dot_general(
            rows, weight[...], (((1,), (1,)), ((), ())), preferred_element_type=F32
        )

    def work(ra, rb):
        for r in (ra, rb):
            for j in range(1, 8):
                hop2(r, j).wait_recv()
        rows = jnp.concatenate([R[ra], R[rb]], axis=0)
        gate = across(rows, wg)
        up = across(rows, wu)
        hidden = (gate / (1.0 + jnp.exp(-gate)) * up).astype(BF)
        result = jnp.dot(hidden, wd[...], preferred_element_type=F32).astype(BF)
        O[ra] = result[:128]
        O[rb] = result[128:]
        M[ra, 0:16] = result[0:16]
        M[rb, 0:16] = result[128:144]
        for r in (rb, ra):
            for j in (4, 5, 2, 6, 3, 7, 1):
                hop3(r, j).start()

    def quarter(r):
        return rcopy(Qs.at[r], Q.at[r], sq.at[r], rq.at[r], opposite(r))

    def weigh(r):
        for j in range(1, 8):
            hop3(r, j).wait_recv()
        w = table(r, gates)
        hi = w.astype(BF)
        lo = (w - hi.astype(F32)).astype(BF)
        dims = (((0,), (0,)), ((), ()))
        sums = lax.dot_general(hi, M[r], dims, preferred_element_type=F32) + lax.dot_general(
            lo, M[r], dims, preferred_element_type=F32
        )
        Qs[r] = sums[96:].astype(BF)
        T[r] = sums[:96]
        quarter(r).start()

    def weigh_pairs(first_one, last_one):
        def one(i, carry):
            weigh(jnp.where(i % 2 == 0, (8 - i // 2) % 8, i // 2 + 1))
            return carry

        lax.fori_loop(first_one, last_one, one, 0)

    def pass_on(s, h):
        for d in (0, 1):

            @pl.when((s < 4) | ((s == 4) & (h == d)))
            def _():
                part = X.at[shard(d, s), pl.ds(0, 3), pl.ds(16 * h, 16)]
                rcopy(part, part, sz.at[d, s - 1, h], rz.at[d, s - 1, h], towards[d]).wait_recv()

            @pl.when((s < 3) | ((s == 3) & (h == d)))
            def _():
                ring(d, s + 1, h).start()

    def step(s, carry):
        @pl.when(s < 5)
        def _():
            pass_on(s, 0)

        @pl.when(s < 6)
        def _():
            fourth((9 - s) % 8).wait_recv()
            spread((9 - s) % 8)

        @pl.when((s > 1) & (s < 5))
        def _():
            fourth(s - 1).wait_recv()
            spread(s - 1)

        @pl.when(s < 5)
        def _():
            pass_on(s, 1)
            fourth((8 - s) % 8).start()

        @pl.when(s < 4)
        def _():
            fourth(s).start()

        @pl.when(s > 2)
        def _():
            work((11 - s) % 8, s - 2)

        @pl.when(s > 4)
        def _():
            weigh_pairs(2 * s - 10, 2 * s - 8)

        return carry

    lax.fori_loop(1, 7, step, 0)

    def joined(r):
        quarter(r).wait_recv()
        T[r, 0:32] = T[r, 0:32] + Q[r].astype(F32)

    def half(h):
        return pl.ds(h * 48, 48)

    def reduce(d, s, h):
        return rcopy(
            sbuf.at[d, s - 1, half(h)], rbuf.at[d, s - 1, half(h)],
            sr.at[d, s - 1, h], rr.at[d, s - 1, h], towards[d],
        )

    weigh_pairs(4, 6)
    weigh(4)
    weigh(5)
    joined(4)
    for d in (0, 1):
        sbuf[d, 0, half(d)] = T[4, half(d)].astype(BF)
    for d in (0, 1):
        reduce(d, 1, d).start()

    def fold(s, carry):
        joined(5 - s)
        joined(3 + s)
        for h in (0, 1):
            for d, r in ((0, 5 - s), (1, 3 + s)):

                @pl.when((s > 2) | (h == d))
                def _():
                    reduce(d, s - 1, h).wait_recv()
                    sbuf[d, s - 1, half(h)] = (
                        T[r, half(h)] + rbuf[d, s - 2, half(h)].astype(F32)
                    ).astype(BF)

                @pl.when((s == 2) & (h != d))
                def _():
                    sbuf[d, s - 1, half(h)] = T[r, half(h)].astype(BF)

            for d in (0, 1):
                reduce(d, s, h).start()
        return carry

    lax.fori_loop(2, 5, fold, 0)
    joined(0)
    for h in (0, 1):
        for d in (0, 1):
            reduce(d, 4, h).wait_recv()
    T[0] = T[0] + rbuf[0, 3].astype(F32) + rbuf[1, 3].astype(F32)
    home[...] = T[0].astype(BF)

    def last(p, k):
        return rcopy(
            home.at[pl.ds(p * 32, 32)], H.at[p], s4.at[p], r4.at[p],
            dev(z, y + (4 - k) * odd, x + (4 - k) * (1 - odd), c),
        )

    total = T[0, 0:32]
    for p, k in ((1, 1), (2, 3)):
        last(p, k).start()
    for p, k in ((1, 1), (2, 3)):
        last(p, k).wait_recv()
        total += H[p].astype(F32)
    out[...] = total

    for p, k in ((1, 1), (2, 3)):
        first(p, k).wait_send()
        last(p, k).wait_send()
    for d in (0, 1):
        for s in (1, 2, 3, 4):
            for h in (0, 1):
                if s < 4 or h == d:
                    ring(d, s, h).wait_send()
                if s > 1 or h == d:
                    reduce(d, s, h).wait_send()

    def drain(r, carry):
        fourth(r).wait_send()
        quarter(r).wait_send()
        for j in range(1, 8):
            hop2(r, j).wait_send()
            hop3(r, j).wait_send()
        return carry

    lax.fori_loop(0, 8, drain, 0)


def experts(own, slots, gates, wg, wu, wd):
    vm = pl.BlockSpec(memory_space=pltpu.VMEM)
    big = pltpu.VMEM((8, 128, 2048), BF)
    dma = pltpu.SemaphoreType.DMA
    return pl.pallas_call(
        experts_kernel,
        out_shape=jax.ShapeDtypeStruct((32, 2048), F32),
        in_specs=[vm] * 6,
        out_specs=vm,
        scratch_shapes=[
            pltpu.VMEM((8, 4, 32, 2048), BF), big, big, big, big,
            pltpu.VMEM((8, 96, 2048), F32),
            pltpu.VMEM((2, 4, 96, 2048), BF),
            pltpu.VMEM((2, 4, 96, 2048), BF),
            pltpu.VMEM((96, 2048), BF),
            pltpu.VMEM((3, 32, 2048), BF),
            pltpu.VMEM((8, 32, 2048), BF),
            pltpu.VMEM((8, 32, 2048), BF),
            dma((4,)), dma((4,)),
            dma((2, 4, 2)), dma((2, 4, 2)),
            dma((8, 8)), dma((8, 8)), dma((8, 8)), dma((8, 8)),
            dma((2, 4, 2)), dma((2, 4, 2)),
            dma((4,)), dma((4,)),
            dma((8,)), dma((8,)), dma((8,)), dma((8,)),
            dma,
        ],
        compiler_params=pltpu.CompilerParams(
            collective_id=4, has_side_effects=True, vmem_limit_bytes=60 * 2**20
        ),
        name="experts",
    )(own, slots, gates, wg, wu, wd)


def slot_tables(rgs, z, y, x, c):
    plane = lax.broadcasted_iota(jnp.int32, (4, 2, 4, 16, 32), 2)
    mine = jnp.where(plane % 2 == 0, rgs[0], rgs[1])
    mine = mine.transpose(1, 2, 0, 3, 4).reshape(8, 4, 16, 32)
    routes = mine[:, :, :6].astype(jnp.int32)
    gates = mine[:, :, 8:14]
    off = jnp.arange(8, dtype=jnp.int32) // 2
    core = (c + jnp.arange(8, dtype=jnp.int32) % 2) % 2
    base = (z // 4) * 32
    along_y = base + ((y + off) % 4) * 8 + x * 2 + core
    along_x = base + y * 8 + ((x + off) % 4) * 2 + core
    u = jnp.arange(8, dtype=jnp.int32)[:, None]
    expert = jnp.where(u % 2 == 0, along_y[None], along_x[None])
    hit = routes[:, :, None] == expert[:, None, :, None, None]
    member = jnp.any(hit, axis=3)
    gate = jnp.sum(jnp.where(hit, gates[:, :, None], 0.0), axis=3)
    ti = lax.broadcasted_iota(jnp.int32, (32, 32), 0)
    tj = lax.broadcasted_iota(jnp.int32, (32, 32), 1)
    before = (ti < tj).astype(BF)
    rank = jnp.dot(
        member.astype(BF).reshape(256, 32), before, preferred_element_type=F32
    ).reshape(8, 4, 8, 32)
    place_ = lax.broadcasted_iota(jnp.int32, (8, 4, 8, 32), 1)
    slot = jnp.where(member, (place_ * 4).astype(F32) + rank, -1.0)
    return slot, gate


def body(
    tokens, block_ids, attn_gain, q_weight, kv_weight, kv_gain, uk_weight, uv_weight,
    o_weight, ffn_gain, w_gate, w_up, w_down, routes, gate_weights,
):
    z, y, x, c = place()
    t = lax.axis_index("tp")
    s = lax.axis_index("seq")
    own_blocks = lax.dynamic_slice(block_ids, (s, 0), (1, 2))[0]
    normed_own = normalize(tokens, attn_gain).astype(BF)
    own_pos = own_blocks[t // 2] * 64 + (t % 2) * 32 + jnp.arange(32, dtype=jnp.int32)
    projected = jnp.dot(normed_own, kv_weight, preferred_element_type=F32)
    latent = normalize(projected[:, :512], kv_gain).astype(BF)
    key_rope = rotate(projected[:, 512:], own_pos).astype(BF)
    kv_own = jnp.concatenate([latent, key_rope, jnp.zeros((32, 64), BF)], axis=1)
    pad2 = jnp.zeros((4, 32, 2), F32)
    rg = jnp.concatenate(
        [
            routes.astype(F32).reshape(4, 32, 6), pad2,
            gate_weights.reshape(4, 32, 6), pad2,
        ],
        axis=2,
    ).transpose(0, 2, 1)
    query_pos = (own_blocks[:, None] * 64 + jnp.arange(64, dtype=jnp.int32)[None, :]).reshape(128)
    frequency = jnp.exp(jnp.arange(32, dtype=F32) * (-2.0 * math.log(10000.0) / 64))
    angles = frequency[:, None] * query_pos.astype(F32)[None, :]
    kv, q, rgs = gather_keys(
        kv_own, normed_own, rg, q_weight, uk_weight, jnp.cos(angles), jnp.sin(angles)
    )
    ids = jnp.arange(64, dtype=jnp.int32)
    inv = jnp.sum(
        jnp.where(block_ids[:, 0][None, :] == ids[:, None], ids[None, :], 0), axis=1
    ).astype(jnp.int32)
    out_latent = attention(inv, own_blocks[:1], q, kv.reshape(64, 128, KEYW))
    out_latent = out_latent.reshape(2, 4, 64, 512).transpose(1, 0, 2, 3).reshape(4, 128, 512)
    head_out = jnp.einsum(
        "htl,hlv->thv", out_latent, uv_weight, preferred_element_type=F32
    ).astype(BF)
    partial_out = jnp.dot(head_out.reshape(128, 512), o_weight, preferred_element_type=F32)
    parts = exchange(
        tp_scatter_kernel, "tp_scatter", 1, partial_out.astype(BF).reshape(4, 32, 2048),
        (4, 32, 2048),
    )
    attn_own = jnp.sum(parts.astype(F32), axis=0)
    mixed = (tokens.astype(F32) + attn_own).astype(BF)
    normed_ffn = normalize(mixed, ffn_gain).astype(BF)
    slots, gates = slot_tables(rgs, z, y, x, c)
    sums = experts(normed_ffn, slots, gates, w_gate[0].T, w_up[0].T, w_down[0])
    return (mixed.astype(F32) + sums).astype(BF)


def solution(mesh):
    return jax.shard_map(
        body,
        mesh=mesh,
        in_specs=(
            P(("seq", "tp"), None), P(), P(), P(None, "tp"), P(), P(),
            P("tp", None, None), P("tp", None, None), P("tp", None), P(),
            P("seq", None, "tp"), P("seq", None, "tp"), P("seq", "tp", None),
            P("seq", None), P("seq", None),
        ),
        out_specs=P(("seq", "tp"), None),
        check_vma=False,
    )
```

```python
import functools
import math

import jax
import jax.numpy as jnp
from jax import lax
from jax.experimental import pallas as pl
from jax.experimental.pallas import tpu as pltpu
from jax.sharding import PartitionSpec as P

EPSILON = 1e-06
MESH = pl.DeviceIdType.MESH
BF = jnp.bfloat16
F32 = jnp.float32
KEYW = 640


def place():
    s = lax.axis_index("seq")
    t = lax.axis_index("tp")
    return (s // 32) * 4 + t, (s // 8) % 4, (s // 2) % 4, s % 2


def dev(z, y, x, c):
    z, y, x, c = z % 8, y % 4, x % 4, c % 2
    return ((z // 4) * 32 + y * 8 + x * 2 + c, z % 4)


def greet(peers):
    barrier = pltpu.get_barrier_semaphore()
    for p in peers:
        pl.semaphore_signal(barrier, inc=1, device_id=p, device_id_type=MESH)
    pl.semaphore_wait(barrier, len(peers))


def rcopy(src, dst, ss, rs, device):
    return pltpu.make_async_remote_copy(
        src_ref=src, dst_ref=dst, send_sem=ss, recv_sem=rs, device_id=device, device_id_type=MESH
    )


def normalize(values, gain_vec):
    values = values.astype(F32)
    factor = lax.rsqrt(jnp.mean(values * values, axis=-1, keepdims=True) + EPSILON)
    return values * factor * gain_vec


def rotate(values, position):
    half_width = values.shape[-1] // 2
    frequency = jnp.exp(
        jnp.arange(half_width, dtype=F32) * (-2.0 * math.log(10000.0) / values.shape[-1])
    )
    angles = position.astype(F32).reshape(position.shape + (1,) * (values.ndim - 1)) * frequency
    cosine = jnp.cos(angles)
    sine_part = jnp.sin(angles)
    first_half = values[..., :half_width]
    second_half = values[..., half_width:]
    return jnp.concatenate(
        [
            first_half * cosine - second_half * sine_part,
            second_half * cosine + first_half * sine_part,
        ],
        axis=-1,
    )


def gather_kernel(
    kv_ref, nt_ref, rg_ref, qw_ref, uk_ref, cos_ref, sin_ref, KV, QO, RG, NT, ssem, rsem, lsem
):
    z, y, x, c = place()
    zh, t = z // 4, z % 4
    peers = [dev(z + k, y, x, c) for k in range(1, 8)]
    xs = [dev(z, y, x + 1, c), dev(z, y, x + 3, c), dev(z, y, x + 2, c)]
    ys = [dev(z, y + 1, x, c), dev(z, y + 3, x, c), dev(z, y + 2, x, c)]
    other = dev(z, y, x, c + 1)
    greet(peers + xs + ys + [other])
    number = [0]
    sent = []

    def send(src, dst, device):
        i = number[0]
        number[0] += 1
        cp = rcopy(src, dst, ssem.at[i], rsem.at[i], device)
        cp.start()
        sent.append(cp)
        return i

    def arrived(i, region):
        rcopy(region, region, ssem.at[i], rsem.at[i], other).wait_recv()

    rows = pl.ds(pl.multiple_of(t * 32, 32), 32)
    zi = {}
    mine = KV.at[zh, y, x, c, rows]
    for k in (4, 3, 5, 2, 6, 1, 7):
        zi[k] = send(kv_ref, mine, dev(z + k, y, x, c))
    locals_ = [
        pltpu.make_async_copy(kv_ref, mine, lsem.at[0]),
        pltpu.make_async_copy(nt_ref, NT.at[t], lsem.at[1]),
        pltpu.make_async_copy(rg_ref, RG.at[0, 0, zh], lsem.at[2]),
    ]
    for cp in locals_:
        cp.start()
    ri = send(rg_ref, RG.at[0, 0, zh], dev(z + 4, y, x, c))
    ti = {}
    for k in (3, 2, 1):
        ti[k] = send(nt_ref, NT.at[t], (zh * 32 + y * 8 + x * 2 + c, (t + k) % 4))
    for cp in locals_:
        cp.wait()
    for k in zi:
        zz = (z - k + 8) % 8
        arrived(zi[k], KV.at[zz // 4, y, x, c, pl.ds(pl.multiple_of((zz % 4) * 32, 32), 32)])
    arrived(ri, RG.at[0, 0, 1 - zh])
    spare = pltpu.make_async_copy(RG.at[0, 0], RG.at[1, 0], lsem.at[2])
    spare.start()
    routes_sent = []
    for p, k in ((1, 1), (2, 3), (3, 2)):
        g = RG.at[0, 0]
        routes_sent.append((send(g, RG.at[0, p], dev(z, y, x + k, c)), RG.at[0, p]))
        routes_sent.append((send(g, RG.at[1, p], dev(z, y + k, x, c)), RG.at[1, p]))
    lo, hi = pl.ds(0, 64), pl.ds(64, 64)
    xm, xp, xo = (x + 3) % 4, (x + 1) % 4, (x + 2) % 4
    ym, yp, yo = (y + 3) % 4, (y + 1) % 4, (y + 2) % 4
    a, b = KV.at[0, y, x, c], KV.at[1, y, x, c]
    ap = send(a, a, xs[0])
    am = send(a, a, xs[1])
    bp = send(b, b, ys[0])
    bm = send(b, b, ys[1])
    arrived(ap, KV.at[0, y, xm, c])
    g = KV.at[0, y, xm, c, lo]
    ap2 = send(g, g, xs[0])
    arrived(bp, KV.at[1, ym, x, c])
    g = KV.at[1, ym, x, c, lo]
    bp2 = send(g, g, ys[0])
    arrived(am, KV.at[0, y, xp, c])
    g = KV.at[0, y, xp, c, hi]
    am2 = send(g, g, xs[1])
    arrived(bm, KV.at[1, yp, x, c])
    g = KV.at[1, yp, x, c, hi]
    bm2 = send(g, g, ys[1])
    arrived(ap2, KV.at[0, y, xo, c, lo])
    arrived(am2, KV.at[0, y, xo, c, hi])
    r = KV.at[0, y, :, c]
    rp = send(r, r, ys[0])
    rm = send(r, r, ys[1])
    arrived(bp2, KV.at[1, yo, x, c, lo])
    arrived(bm2, KV.at[1, yo, x, c, hi])
    q = KV.at[1, :, x, c]
    qp = send(q, q, xs[0])
    qm = send(q, q, xs[1])
    across = [send(r, r, other), send(q, q, other)]
    for k in ti:
        arrived(ti[k], NT.at[(t - k + 4) % 4])
    queries = jnp.dot(
        NT[...].reshape(128, 2048), qw_ref[...], preferred_element_type=F32
    ).T.astype(BF)
    lane = lax.broadcasted_iota(jnp.int32, (576, 128), 1)
    for pair in (0, 1):
        heads = []
        for h in (2 * pair, 2 * pair + 1):
            at = h * 192
            long = jnp.dot(uk_ref[h], queries[at : at + 128], preferred_element_type=F32)
            one = queries[at + 128 : at + 160].astype(F32)
            two = queries[at + 160 : at + 192].astype(F32)
            turned = [one * cos_ref[...] - two * sin_ref[...],
                      two * cos_ref[...] + one * sin_ref[...]]
            heads.append(jnp.concatenate([long] + turned, axis=0))
        cols = pl.ds(pair * 128, 128)
        QO[0, 0:576, cols] = jnp.where(lane < 64, heads[0], pltpu.roll(heads[1], 64, 1)).astype(BF)
        QO[1, 0:576, cols] = jnp.where(lane < 64, pltpu.roll(heads[0], 64, 1), heads[1]).astype(BF)
    QO[:, 576:640, :] = jnp.zeros((2, 64, 256), BF)
    arrived(rp, KV.at[0, ym, :, c])
    g = KV.at[0, ym, :, c, lo]
    rp2 = send(g, g, ys[0])
    arrived(qp, KV.at[1, :, xm, c])
    g = KV.at[1, :, xm, c, lo]
    qp2 = send(g, g, xs[0])
    arrived(rm, KV.at[0, yp, :, c])
    g = KV.at[0, yp, :, c, hi]
    rm2 = send(g, g, ys[1])
    arrived(qm, KV.at[1, :, xp, c])
    g = KV.at[1, :, xp, c, hi]
    qm2 = send(g, g, xs[1])
    for g in (KV.at[0, ym, :, c], KV.at[1, :, xm, c], KV.at[0, yp, :, c], KV.at[1, :, xp, c]):
        across.append(send(g, g, other))
    arrived(rp2, KV.at[0, yo, :, c, lo])
    arrived(rm2, KV.at[0, yo, :, c, hi])
    g = KV.at[0, yo, :, c]
    across.append(send(g, g, other))
    arrived(qp2, KV.at[1, :, xo, c, lo])
    arrived(qm2, KV.at[1, :, xo, c, hi])
    g = KV.at[1, :, xo, c]
    across.append(send(g, g, other))
    d = 1 - c
    for i, region in zip(
        across,
        (
            KV.at[0, y, :, d],
            KV.at[1, :, x, d],
            KV.at[0, ym, :, d],
            KV.at[1, :, xm, d],
            KV.at[0, yp, :, d],
            KV.at[1, :, xp, d],
            KV.at[0, yo, :, d],
            KV.at[1, :, xo, d],
        ),
    ):
        arrived(i, region)
    spare.wait()
    for i, region in routes_sent:
        arrived(i, region)
    for cp in sent:
        cp.wait_send()


def gather_keys(kv_own, normed_own, rg, qw, uk, cosine, sine):
    count = 48
    vm = pl.BlockSpec(memory_space=pltpu.VMEM)
    return pl.pallas_call(
        gather_kernel,
        out_shape=(
            jax.ShapeDtypeStruct((2, 4, 4, 2, 128, KEYW), BF),
            jax.ShapeDtypeStruct((2, KEYW, 256), BF),
            jax.ShapeDtypeStruct((2, 4, 2, 4, 16, 32), F32),
        ),
        in_specs=[vm] * 7,
        out_specs=(pl.BlockSpec(memory_space=pltpu.HBM), vm, vm),
        scratch_shapes=[
            pltpu.VMEM((4, 32, 2048), BF),
            pltpu.SemaphoreType.DMA((count,)),
            pltpu.SemaphoreType.DMA((count,)),
            pltpu.SemaphoreType.DMA((3,)),
        ],
        compiler_params=pltpu.CompilerParams(
            collective_id=0, has_side_effects=True, vmem_limit_bytes=60 * 2**20
        ),
        name="gather_keys",
    )(kv_own, normed_own, rg, qw, uk, cosine, sine)


CHUNK = 1024


def attention_kernel(inv_ref, blk_ref, q_ref, kv_hbm, o_ref, kbuf, m_ref, l_ref, acc_ref, sems):
    low = blk_ref[0]
    per = CHUNK // 64
    top_chunks = (127 - low) // per + 1

    def issue(p, carry):
        second = p >= 64
        d = inv_ref[jnp.where(second, 127 - p, p)]
        off = pl.multiple_of(jnp.where(second, 64, 0), 64)
        pltpu.make_async_copy(
            kv_hbm.at[d, pl.ds(off, 64)],
            kbuf.at[pl.ds(pl.multiple_of(p * 64, 64), 64)],
            sems.at[p // per],
        ).start()
        return carry

    lax.fori_loop(0, top_chunks * per, issue, 0)
    scale = (128 + 64) ** (-0.5)

    for half in (1, 0):
        block = low if half == 0 else 127 - low
        last = block // per
        m_ref[...] = jnp.full_like(m_ref, -1e30)
        l_ref[...] = jnp.zeros_like(l_ref)
        acc_ref[...] = jnp.zeros_like(acc_ref)

        def step(ch, masked):
            region = kbuf.at[pl.ds(pl.multiple_of(ch * CHUNK, CHUNK), CHUNK)]
            if half == 1:
                pltpu.make_async_copy(region, region, sems.at[ch]).wait()
            keys = region[...]
            s = jnp.dot(keys, q_ref[half], preferred_element_type=F32) * scale
            if masked:
                key = lax.broadcasted_iota(jnp.int32, s.shape, 0)
                query = lax.broadcasted_iota(jnp.int32, s.shape, 1) % 64
                s = jnp.where(key - query <= block * 64 - ch * CHUNK, s, -1e30)
            m_old = m_ref[...]
            m_new = jnp.maximum(m_old, jnp.max(s, axis=0, keepdims=True))
            p = jnp.exp(s - m_new)
            alpha = jnp.exp(m_old - m_new)
            l_ref[...] = l_ref[...] * alpha + jnp.sum(p, axis=0, keepdims=True)
            m_ref[...] = m_new
            acc_ref[...] = acc_ref[...] * alpha + lax.dot_general(
                keys[:, :512], p.astype(BF), (((0,), (0,)), ((), ())), preferred_element_type=F32
            )

        def loop(ch, carry):
            step(ch, False)
            return carry

        lax.fori_loop(0, last, loop, 0)
        step(last, True)
        o_ref[half] = (acc_ref[...] / l_ref[...]).T.astype(BF)


def attention(inv, low, q, kv):
    return pl.pallas_call(
        attention_kernel,
        out_shape=jax.ShapeDtypeStruct((2, 256, 512), BF),
        in_specs=[
            pl.BlockSpec(memory_space=pltpu.SMEM),
            pl.BlockSpec(memory_space=pltpu.SMEM),
            pl.BlockSpec(memory_space=pltpu.VMEM),
            pl.BlockSpec(memory_space=pltpu.HBM),
        ],
        out_specs=pl.BlockSpec(memory_space=pltpu.VMEM),
        scratch_shapes=[
            pltpu.VMEM((8192, KEYW), BF),
            pltpu.VMEM((1, 256), F32),
            pltpu.VMEM((1, 256), F32),
            pltpu.VMEM((512, 256), F32),
            pltpu.SemaphoreType.DMA((8192 // CHUNK,)),
        ],
        compiler_params=pltpu.CompilerParams(vmem_limit_bytes=60 * 2**20),
        name="attention",
    )(inv, low, q, kv)


def tp_scatter_kernel(p_ref, o_ref, ssem, rsem, lsem):
    z, y, x, c = place()
    s, t = lax.axis_index("seq"), lax.axis_index("tp")
    greet([(s, (t + k) % 4) for k in (1, 2, 3)])
    cps = []
    for k in (2, 3, 1):
        to = (t + k) % 4
        cp = rcopy(p_ref.at[to], o_ref.at[k], ssem.at[k], rsem.at[k], (s, to))
        cp.start()
        cps.append(cp)
    own = pltpu.make_async_copy(p_ref.at[t], o_ref.at[0], lsem)
    own.start()
    own.wait()
    for cp in cps:
        cp.wait()


def exchange(kernel, name, cid, array, out):
    vm = pl.BlockSpec(memory_space=pltpu.VMEM)
    return pl.pallas_call(
        kernel,
        out_shape=jax.ShapeDtypeStruct(out, BF),
        in_specs=[vm],
        out_specs=vm,
        scratch_shapes=[
            pltpu.SemaphoreType.DMA((8,)),
            pltpu.SemaphoreType.DMA((8,)),
            pltpu.SemaphoreType.DMA,
        ],
        compiler_params=pltpu.CompilerParams(
            collective_id=cid, has_side_effects=True, vmem_limit_bytes=16 * 2**20
        ),
        name=name,
    )(array)


def experts_kernel(
    own, slots, gates, wg, wu, wd, out,
    X, S, R, O, M, T, rbuf, sbuf, home, H, Qs, Q,
    sx, rx, sz, rz, s2, r2, s3, r3, sr, rr, s4, r4, sf, rf, sq, rq, lsem,
):
    z, y, x, c = place()
    towards = [dev(z + 1, y, x, c), dev(z + 7, y, x, c)]
    peers = towards + [dev(z, y, x, c + 1)]
    for k in (1, 2, 3):
        for d in (0, 1):
            peers.append(dev(z, y + k, x, c + d))
            peers.append(dev(z, y, x + k, c + d))
    greet(peers)
    odd = z % 2

    def first(p, k):
        return rcopy(
            own, X.at[z, p], sx.at[p], rx.at[p], dev(z, y + k * odd, x + k * (1 - odd), c)
        )

    def opposite(r):
        o = (z + r) % 2
        return dev(z, y + 2 * o, x + 2 * (1 - o), c)

    for p, k in ((1, 1), (2, 3)):
        first(p, k).start()
    here = pltpu.make_async_copy(own, X.at[z, 0], lsem)
    here.start()

    def shard(d, s):
        return (z + 8 - s) % 8 if d == 0 else (z + s) % 8

    def ring(d, s, h):
        part = X.at[shard(d, s - 1), pl.ds(0, 3), pl.ds(16 * h, 16)]
        return rcopy(part, part, sz.at[d, s - 1, h], rz.at[d, s - 1, h], towards[d])

    def fourth(r):
        u = (z + r) % 8
        return rcopy(X.at[u, 0], X.at[u, 3], sf.at[r], rf.at[r], opposite(r))

    here.wait()
    first(1, 1).wait_recv()
    first(2, 3).wait_recv()
    for h in (0, 1):
        for d in (0, 1):
            ring(d, 1, h).start()
    fourth(0).start()

    def rows16(j):
        return pl.ds(j * 16, 16)

    def partner(r, j, sign):
        o = (z + r) % 2
        step = (j // 2) * sign + 4
        return dev(z, y + step * (1 - o), x + step * o, c + j % 2)

    def hop2(r, j):
        return rcopy(
            S.at[r, rows16(j)], R.at[r, rows16(j)], s2.at[r, j], r2.at[r, j], partner(r, j, 1)
        )

    def hop3(r, j):
        return rcopy(
            O.at[r, rows16(j)], M.at[r, rows16(j)], s3.at[r, j], r3.at[r, j], partner(r, j, -1)
        )

    number = lax.broadcasted_iota(jnp.int32, (8, 16, 32), 1).astype(F32)

    def table(r, scale=None):
        u = (z + r) % 8
        parts = []
        for p in range(4):
            part = (slots[u, p][:, None, :] == number).astype(F32)
            if scale is not None:
                part = part * scale[u, p][:, None, :]
            parts.append(part.reshape(128, 32))
        return jnp.concatenate(parts, axis=1)

    def spread(r):
        tokens = X[(z + r) % 8].reshape(128, 2048)
        S[r] = jnp.dot(
            table(r).astype(BF), tokens, preferred_element_type=F32
        ).astype(BF)
        for j in (4, 5, 2, 6, 3, 7, 1):
            hop2(r, j).start()
        R[r, 0:16] = S[r, 0:16]

    def across(rows, weight):
        return lax.dot_general(
            rows, weight[...], (((1,), (1,)), ((), ())), preferred_element_type=F32
        )

    def work(ra, rb):
        for r in (ra, rb):
            for j in range(1, 8):
                hop2(r, j).wait_recv()
        rows = jnp.concatenate([R[ra], R[rb]], axis=0)
        gate = across(rows, wg)
        up = across(rows, wu)
        hidden = (gate / (1.0 + jnp.exp(-gate)) * up).astype(BF)
        result = jnp.dot(hidden, wd[...], preferred_element_type=F32).astype(BF)
        O[ra] = result[:128]
        O[rb] = result[128:]
        M[ra, 0:16] = result[0:16]
        M[rb, 0:16] = result[128:144]
        for r in (rb, ra):
            for j in (4, 5, 2, 6, 3, 7, 1):
                hop3(r, j).start()

    def pass_on(s, h):
        for d in (0, 1):

            @pl.when((s < 4) | ((s == 4) & (h == d)))
            def _():
                part = X.at[shard(d, s), pl.ds(0, 3), pl.ds(16 * h, 16)]
                rcopy(part, part, sz.at[d, s - 1, h], rz.at[d, s - 1, h], towards[d]).wait_recv()

            @pl.when((s < 3) | ((s == 3) & (h == d)))
            def _():
                ring(d, s + 1, h).start()

    def step(s, carry):
        @pl.when(s < 5)
        def _():
            pass_on(s, 0)

        @pl.when(s < 6)
        def _():
            fourth((9 - s) % 8).wait_recv()
            spread((9 - s) % 8)

        @pl.when((s > 1) & (s < 5))
        def _():
            fourth(s - 1).wait_recv()
            spread(s - 1)

        @pl.when(s < 5)
        def _():
            pass_on(s, 1)
            fourth((8 - s) % 8).start()

        @pl.when(s < 4)
        def _():
            fourth(s).start()

        @pl.when(s > 2)
        def _():
            work((11 - s) % 8, s - 2)

        return carry

    lax.fori_loop(1, 7, step, 0)

    def quarter(r):
        return rcopy(Qs.at[r], Q.at[r], sq.at[r], rq.at[r], opposite(r))

    def weigh(r):
        for j in range(1, 8):
            hop3(r, j).wait_recv()
        w = table(r, gates)
        hi = w.astype(BF)
        lo = (w - hi.astype(F32)).astype(BF)
        dims = (((0,), (0,)), ((), ()))
        sums = lax.dot_general(hi, M[r], dims, preferred_element_type=F32) + lax.dot_general(
            lo, M[r], dims, preferred_element_type=F32
        )
        Qs[r] = sums[96:].astype(BF)
        T[r] = sums[:96]
        quarter(r).start()

    def joined(r):
        quarter(r).wait_recv()
        T[r, 0:32] = T[r, 0:32] + Q[r].astype(F32)

    def half(h):
        return pl.ds(h * 48, 48)

    def reduce(d, s, h):
        return rcopy(
            sbuf.at[d, s - 1, half(h)], rbuf.at[d, s - 1, half(h)],
            sr.at[d, s - 1, h], rr.at[d, s - 1, h], towards[d],
        )

    weigh(4)
    weigh(5)
    joined(4)
    for d in (0, 1):
        sbuf[d, 0, half(d)] = T[4, half(d)].astype(BF)
    for d in (0, 1):
        reduce(d, 1, d).start()
    weigh(3)

    def fold(s, carry):
        joined(5 - s)
        joined(3 + s)
        for h in (0, 1):
            for d, r in ((0, 5 - s), (1, 3 + s)):

                @pl.when((s > 2) | (h == d))
                def _():
                    reduce(d, s - 1, h).wait_recv()
                    sbuf[d, s - 1, half(h)] = (
                        T[r, half(h)] + rbuf[d, s - 2, half(h)].astype(F32)
                    ).astype(BF)

                @pl.when((s == 2) & (h != d))
                def _():
                    sbuf[d, s - 1, half(h)] = T[r, half(h)].astype(BF)

            for d in (0, 1):
                reduce(d, s, h).start()
        weigh(4 - s)

        @pl.when(s < 4)
        def _():
            weigh(4 + s)

        return carry

    lax.fori_loop(2, 5, fold, 0)
    joined(0)
    for h in (0, 1):
        for d in (0, 1):
            reduce(d, 4, h).wait_recv()
    T[0] = T[0] + rbuf[0, 3].astype(F32) + rbuf[1, 3].astype(F32)
    home[...] = T[0].astype(BF)

    def last(p, k):
        return rcopy(
            home.at[pl.ds(p * 32, 32)], H.at[p], s4.at[p], r4.at[p],
            dev(z, y + (4 - k) * odd, x + (4 - k) * (1 - odd), c),
        )

    total = T[0, 0:32]
    for p, k in ((1, 1), (2, 3)):
        last(p, k).start()
    for p, k in ((1, 1), (2, 3)):
        last(p, k).wait_recv()
        total += H[p].astype(F32)
    out[...] = total

    for p, k in ((1, 1), (2, 3)):
        first(p, k).wait_send()
        last(p, k).wait_send()
    for d in (0, 1):
        for s in (1, 2, 3, 4):
            for h in (0, 1):
                if s < 4 or h == d:
                    ring(d, s, h).wait_send()
                if s > 1 or h == d:
                    reduce(d, s, h).wait_send()

    def drain(r, carry):
        fourth(r).wait_send()
        quarter(r).wait_send()
        for j in range(1, 8):
            hop2(r, j).wait_send()
            hop3(r, j).wait_send()
        return carry

    lax.fori_loop(0, 8, drain, 0)


def experts(own, slots, gates, wg, wu, wd):
    vm = pl.BlockSpec(memory_space=pltpu.VMEM)
    big = pltpu.VMEM((8, 128, 2048), BF)
    dma = pltpu.SemaphoreType.DMA
    return pl.pallas_call(
        experts_kernel,
        out_shape=jax.ShapeDtypeStruct((32, 2048), F32),
        in_specs=[vm] * 6,
        out_specs=vm,
        scratch_shapes=[
            pltpu.VMEM((8, 4, 32, 2048), BF), big, big, big, big,
            pltpu.VMEM((8, 96, 2048), F32),
            pltpu.VMEM((2, 4, 96, 2048), BF),
            pltpu.VMEM((2, 4, 96, 2048), BF),
            pltpu.VMEM((96, 2048), BF),
            pltpu.VMEM((3, 32, 2048), BF),
            pltpu.VMEM((8, 32, 2048), BF),
            pltpu.VMEM((8, 32, 2048), BF),
            dma((4,)), dma((4,)),
            dma((2, 4, 2)), dma((2, 4, 2)),
            dma((8, 8)), dma((8, 8)), dma((8, 8)), dma((8, 8)),
            dma((2, 4, 2)), dma((2, 4, 2)),
            dma((4,)), dma((4,)),
            dma((8,)), dma((8,)), dma((8,)), dma((8,)),
            dma,
        ],
        compiler_params=pltpu.CompilerParams(
            collective_id=4, has_side_effects=True, vmem_limit_bytes=60 * 2**20
        ),
        name="experts",
    )(own, slots, gates, wg, wu, wd)


def slot_tables(rgs, z, y, x, c):
    plane = lax.broadcasted_iota(jnp.int32, (4, 2, 4, 16, 32), 2)
    mine = jnp.where(plane % 2 == 0, rgs[0], rgs[1])
    mine = mine.transpose(1, 2, 0, 3, 4).reshape(8, 4, 16, 32)
    routes = mine[:, :, :6].astype(jnp.int32)
    gates = mine[:, :, 8:14]
    off = jnp.arange(8, dtype=jnp.int32) // 2
    core = (c + jnp.arange(8, dtype=jnp.int32) % 2) % 2
    base = (z // 4) * 32
    along_y = base + ((y + off) % 4) * 8 + x * 2 + core
    along_x = base + y * 8 + ((x + off) % 4) * 2 + core
    u = jnp.arange(8, dtype=jnp.int32)[:, None]
    expert = jnp.where(u % 2 == 0, along_y[None], along_x[None])
    hit = routes[:, :, None] == expert[:, None, :, None, None]
    member = jnp.any(hit, axis=3)
    gate = jnp.sum(jnp.where(hit, gates[:, :, None], 0.0), axis=3)
    ti = lax.broadcasted_iota(jnp.int32, (32, 32), 0)
    tj = lax.broadcasted_iota(jnp.int32, (32, 32), 1)
    before = (ti < tj).astype(BF)
    rank = jnp.dot(
        member.astype(BF).reshape(256, 32), before, preferred_element_type=F32
    ).reshape(8, 4, 8, 32)
    place_ = lax.broadcasted_iota(jnp.int32, (8, 4, 8, 32), 1)
    slot = jnp.where(member, (place_ * 4).astype(F32) + rank, -1.0)
    return slot, gate


def body(
    tokens, block_ids, attn_gain, q_weight, kv_weight, kv_gain, uk_weight, uv_weight,
    o_weight, ffn_gain, w_gate, w_up, w_down, routes, gate_weights,
):
    z, y, x, c = place()
    t = lax.axis_index("tp")
    s = lax.axis_index("seq")
    own_blocks = lax.dynamic_slice(block_ids, (s, 0), (1, 2))[0]
    normed_own = normalize(tokens, attn_gain).astype(BF)
    own_pos = own_blocks[t // 2] * 64 + (t % 2) * 32 + jnp.arange(32, dtype=jnp.int32)
    projected = jnp.dot(normed_own, kv_weight, preferred_element_type=F32)
    latent = normalize(projected[:, :512], kv_gain).astype(BF)
    key_rope = rotate(projected[:, 512:], own_pos).astype(BF)
    kv_own = jnp.concatenate([latent, key_rope, jnp.zeros((32, 64), BF)], axis=1)
    pad2 = jnp.zeros((4, 32, 2), F32)
    rg = jnp.concatenate(
        [
            routes.astype(F32).reshape(4, 32, 6), pad2,
            gate_weights.reshape(4, 32, 6), pad2,
        ],
        axis=2,
    ).transpose(0, 2, 1)
    query_pos = (own_blocks[:, None] * 64 + jnp.arange(64, dtype=jnp.int32)[None, :]).reshape(128)
    frequency = jnp.exp(jnp.arange(32, dtype=F32) * (-2.0 * math.log(10000.0) / 64))
    angles = frequency[:, None] * query_pos.astype(F32)[None, :]
    kv, q, rgs = gather_keys(
        kv_own, normed_own, rg, q_weight, uk_weight, jnp.cos(angles), jnp.sin(angles)
    )
    ids = jnp.arange(64, dtype=jnp.int32)
    inv = jnp.sum(
        jnp.where(block_ids[:, 0][None, :] == ids[:, None], ids[None, :], 0), axis=1
    ).astype(jnp.int32)
    out_latent = attention(inv, own_blocks[:1], q, kv.reshape(64, 128, KEYW))
    out_latent = out_latent.reshape(2, 4, 64, 512).transpose(1, 0, 2, 3).reshape(4, 128, 512)
    head_out = jnp.einsum(
        "htl,hlv->thv", out_latent, uv_weight, preferred_element_type=F32
    ).astype(BF)
    partial_out = jnp.dot(head_out.reshape(128, 512), o_weight, preferred_element_type=F32)
    parts = exchange(
        tp_scatter_kernel, "tp_scatter", 1, partial_out.astype(BF).reshape(4, 32, 2048),
        (4, 32, 2048),
    )
    attn_own = jnp.sum(parts.astype(F32), axis=0)
    mixed = (tokens.astype(F32) + attn_own).astype(BF)
    normed_ffn = normalize(mixed, ffn_gain).astype(BF)
    slots, gates = slot_tables(rgs, z, y, x, c)
    sums = experts(normed_ffn, slots, gates, w_gate[0].T, w_up[0].T, w_down[0])
    return (mixed.astype(F32) + sums).astype(BF)


def solution(mesh):
    return jax.shard_map(
        body,
        mesh=mesh,
        in_specs=(
            P(("seq", "tp"), None), P(), P(), P(None, "tp"), P(), P(),
            P("tp", None, None), P("tp", None, None), P("tp", None), P(),
            P("seq", None, "tp"), P("seq", None, "tp"), P("seq", "tp", None),
            P("seq", None), P("seq", None),
        ),
        out_specs=P(("seq", "tp"), None),
        check_vma=False,
    )
```
